32 devices in a mesh: grp: 8 (over z, core), dom: 4 (over y, x).
Axes of the slice: x: 2, y: 2, z: 4, core: 2. Of those that a mesh axis runs over, the one named last changes fastest.
Arguments:
- query: bfloat16 [8192, 512], P(('grp', 'dom')), may hold values from -9 to 9
- key: bfloat16 [8192, 512], P(('grp', 'dom')), may hold values from -6 to 6
- value: bfloat16 [8192, 512], P(('grp', 'dom')), may hold values from -6 to 6
- cotangent: bfloat16 [8192, 512], P(('grp', 'dom')), may hold values from -6 to 6
- tile_index: int32 [32, 8, 3], P(('grp', 'dom')), may hold values from 0 to 3, as said below
- tile_mask: int32 [32, 8, 128, 128], P(('grp', 'dom')), may hold values 0 or 1
- tile_count: int32 [32], P(('grp', 'dom')), may hold values from 1 to 8, as said below
- partner: int32 [32, 4], P(('grp', 'dom')), may hold values from 0 to 31, as said below
- pair_edges: int32 [32, 4, 64, 2], P(('grp', 'dom')), may hold values from 0 to 255, as said below
Outputs:
- attended: bfloat16 [8192, 512], P(('grp', 'dom'))
- grad_query: bfloat16 [8192, 512], P(('grp', 'dom'))
- grad_key: bfloat16 [8192, 512], P(('grp', 'dom'))
- grad_value: bfloat16 [8192, 512], P(('grp', 'dom'))
The draws below stay inside these ranges and needn't reach their ends.
Inputs may be any that keep to these rules, and one draw needn't show every extreme that they name: `tile_index`: the slots of one partition name distinct triples (a, c, b) with a and b below 2 and c below 4. Slots at or beyond tile_count[P] are padding; one partition uses all 8 slots. partner[P, m] has P's domain index, and its group index is P's group index XOR a nonzero code that depends on m only; the 4 codes are distinct and one of them is 4. pair_edges[partner[P, m], m, e] is pair_edges[P, m, e] with its two entries swapped.
All inputs are finite; a program needn't handle non-finite values. No bound on the sum of `tile_mask` on one device may be relied on, other than what follows from the above.
Results may differ from the reference program's by a relative error of at most 0.0075.
The reference program's roundings to bfloat16 on the way count: a program that leaves them out, or rounds other values in their place, can miss the bound.
Values may be sent and summed in bfloat16 or wider, within the bound.
A program may use at most 128 MiB of HBM per device.

```python
import math
import jax
import jax.numpy as jnp
from jax import lax

D = 512
HEADS = 8
HEAD_DIM = 64
NODE_DEV = 256
TILE = 128
MATCH = 4
GROUPS = 8
DOMAINS = 4
PARTS_SIZE = 32
NODES = 8192
ROW_BLOCKS = 2
TILE_SLOTS = 8
EXPANDER = 64


def draw_key(key, part):
    noise = jax.random.normal(jax.random.fold_in(key, 31), (NODES, D), jnp.float32)
    values = jnp.clip(noise, -6.0, 6.0)
    return values.astype(jnp.bfloat16)


def draw_query(key, part):
    noise = jax.random.normal(jax.random.fold_in(key, 37), (NODES, D), jnp.float32)
    values = jnp.clip(noise, -6.0, 6.0)
    return values.astype(jnp.bfloat16)


def draw_tile_index(key, part):
    combos = DOMAINS * ROW_BLOCKS * ROW_BLOCKS

    def one_part(part_id):
        ordering = jax.random.permutation(jax.random.fold_in(jax.random.fold_in(key, 17), part_id), combos)[:TILE_SLOTS]
        return jnp.stack([ordering // (DOMAINS * ROW_BLOCKS), ordering // ROW_BLOCKS % DOMAINS, ordering % ROW_BLOCKS], axis=1)
    return jax.vmap(one_part)(jnp.arange(PARTS_SIZE, dtype=jnp.int32)).astype(jnp.int32)


def draw_tile_count(key, part):
    base_count = 1 + jax.random.randint(jax.random.fold_in(key, 19), (PARTS_SIZE,), 0, TILE_SLOTS // 2)
    heaviest = jax.random.randint(jax.random.fold_in(key, 23), (), 0, PARTS_SIZE)
    return jnp.where(jnp.arange(PARTS_SIZE, dtype=jnp.int32) == heaviest, TILE_SLOTS, base_count).astype(jnp.int32)


def matching_codes(key):
    half_code = GROUPS // 2
    others = jax.random.permutation(jax.random.fold_in(key, 11), GROUPS - 2)[:MATCH - 1] + 1
    others = jnp.where(others >= half_code, others + 1, others)
    codes = jnp.concatenate([jnp.full((1,), half_code, jnp.int32), others.astype(jnp.int32)])
    return jax.random.permutation(jax.random.fold_in(key, 7), codes).astype(jnp.int32)


def draw_partner(key, part):
    match_codes = matching_codes(key)
    part_ids = jnp.arange(PARTS_SIZE, dtype=jnp.int32)
    group_ids = part_ids // DOMAINS
    domain_ids = part_ids % DOMAINS
    return (jnp.bitwise_xor(group_ids[:, None], match_codes[None, :]) * DOMAINS + domain_ids[:, None]).astype(jnp.int32)


def draw_pair_edges(key, part):
    partners = draw_partner(key, part)
    part_ids = jnp.arange(PARTS_SIZE, dtype=jnp.int32)
    lower = jnp.minimum(part_ids[:, None], partners)
    identity = jnp.arange(MATCH, dtype=jnp.int32)[None, :] * PARTS_SIZE + lower

    def one_pair(pair_id):
        return jax.random.randint(jax.random.fold_in(jax.random.fold_in(key, 13), pair_id), (EXPANDER, 2), 0, NODE_DEV)
    pairs = jax.vmap(jax.vmap(one_pair))(identity)
    is_lower = (part_ids[:, None] < partners)[:, :, None, None]
    return jnp.where(is_lower, pairs, pairs[..., ::-1]).astype(jnp.int32)


def plant(array, rng, low, high):
    spot = [jax.random.randint(jax.random.fold_in(rng, axis), (), 0, length) for axis, length in enumerate(array.shape)]
    main_axis = array.shape.index(max(array.shape))
    beside = spot[:main_axis] + [(spot[main_axis] + 1) % array.shape[main_axis]] + spot[main_axis + 1:]
    return array.at[tuple(spot)].set(low).at[tuple(beside)].set(high)


def shard_levels(stream_key, dims, pieces, smallest, largest):
    gain = 1.0
    for axis_at, parts in pieces:
        heights = jax.random.uniform(jax.random.fold_in(jax.random.fold_in(stream_key, 6), axis_at), (parts,), jnp.float32, smallest / len(pieces), largest / len(pieces))
        gain = gain * jnp.repeat(jnp.exp(heights), dims[axis_at] // parts).reshape((-1,) + (1,) * (len(dims) - 1 - axis_at))
    return gain


def centred(key, shape, spread, limit, shards=(), held_as=jnp.bfloat16):
    values = spread * jax.random.normal(key, shape, jnp.float32)
    if shards:
        values = values * shard_levels(key, shape, shards, -0.22, 0.18)
    return jnp.clip(values, -limit, limit).astype(held_as)


def setup_inputs(seed: int = 0) -> dict:
    key_list = jax.random.split(jax.random.key(seed), 10)
    query = draw_query(jax.random.fold_in(key_list[9], 71), 0)
    key = draw_key(jax.random.fold_in(key_list[9], 71), 0)
    value = centred(key_list[2], (NODES, D), 1.0, 6.0, ((0, 32),))
    cotangent = centred(key_list[3], (NODES, D), 1.0, 6.0, ((0, 32),))
    tile_index = draw_tile_index(jax.random.fold_in(key_list[9], 71), 0)
    tile_mask = plant((jax.random.randint(key_list[5], (PARTS_SIZE, TILE_SLOTS, TILE, TILE), 0, TILE // 2) < 1).astype(jnp.int32), jax.random.fold_in(key_list[5], 1), 0, 1)
    tile_count = draw_tile_count(jax.random.fold_in(key_list[9], 71), 0)
    partner = draw_partner(jax.random.fold_in(key_list[9], 71), 0)
    pair_edges = draw_pair_edges(jax.random.fold_in(key_list[9], 71), 0)
    return dict(query=query, key=key, value=value, cotangent=cotangent, tile_index=tile_index, tile_mask=tile_mask, tile_count=tile_count, partner=partner, pair_edges=pair_edges)


def rounded(values):
    return lax.optimization_barrier(values.astype(jnp.bfloat16)).astype(jnp.float32)

def split_heads(values):
    return values.astype(jnp.float32).reshape(values.shape[0], HEADS, HEAD_DIM)

def reference(query, key, value, cotangent, tile_index, tile_mask, tile_count, partner, pair_edges):
    score_scale = 1.0 / math.sqrt(HEAD_DIM)
    group_size = DOMAINS * NODE_DEV
    lane_ids = jnp.arange(TILE, dtype=jnp.int32)
    slot_ids = jnp.arange(TILE_SLOTS, dtype=jnp.int32)

    def part_step(carried, part_id):
        key_acc, value_acc = carried
        own_start = (part_id * NODE_DEV).astype(jnp.int32)
        group_start = (part_id // DOMAINS * group_size).astype(jnp.int32)
        own_query = split_heads(lax.dynamic_slice_in_dim(query, own_start, NODE_DEV, 0))
        own_key = split_heads(lax.dynamic_slice_in_dim(key, own_start, NODE_DEV, 0))
        own_value = split_heads(lax.dynamic_slice_in_dim(value, own_start, NODE_DEV, 0))
        own_grad = split_heads(lax.dynamic_slice_in_dim(cotangent, own_start, NODE_DEV, 0))
        group_key = split_heads(lax.dynamic_slice_in_dim(key, group_start, group_size, 0))
        group_value = split_heads(lax.dynamic_slice_in_dim(value, group_start, group_size, 0))
        entries = tile_index[part_id]
        live_mask = (tile_mask[part_id] != 0) & (slot_ids < tile_count[part_id])[:, None, None]
        row_ids = entries[:, 0:1] * TILE + lane_ids[None, :]
        col_ids = entries[:, 1:2] * NODE_DEV + entries[:, 2:3] * TILE + lane_ids[None, :]
        flat_rows = row_ids.reshape(-1)
        flat_cols = col_ids.reshape(-1)
        tile_query = own_query[row_ids]
        tile_grad = own_grad[row_ids]
        tile_key = group_key[col_ids]
        tile_value = group_value[col_ids]
        tile_score = jnp.einsum('sihe,sjhe->shij', tile_query, tile_key) * score_scale
        tile_score = jnp.where(live_mask[:, None], tile_score, -jnp.inf)
        self_score = lax.optimization_barrier(jnp.sum(own_query * own_key, axis=2)) * score_scale
        partner_ids = partner[part_id]
        near_rows = pair_edges[part_id, :, :, 0].reshape(-1)
        far_rows = (partner_ids[:, None] * NODE_DEV + pair_edges[part_id, :, :, 1]).reshape(-1)
        far_key = split_heads(key[far_rows])
        far_value = split_heads(value[far_rows])
        near_query = own_query[near_rows]
        near_grad = own_grad[near_rows]
        pair_score = lax.optimization_barrier(jnp.sum(near_query * far_key, axis=2)) * score_scale

        def per_row(values):
            return values.transpose(0, 2, 1).reshape(-1, HEADS)

        def tile_rows(values):
            return values[row_ids].transpose(0, 2, 1)[:, :, :, None]
        row_top = self_score.at[flat_rows].max(per_row(lax.optimization_barrier(jnp.max(tile_score, axis=3))))
        row_top = row_top.at[near_rows].max(pair_score)
        tile_exp = jnp.exp(tile_score - tile_rows(row_top))
        self_exp = jnp.exp(self_score - row_top)
        pair_exp = jnp.exp(pair_score - row_top[near_rows])
        row_total = self_exp.at[flat_rows].add(per_row(lax.optimization_barrier(jnp.sum(tile_exp, axis=3))))
        row_total = row_total.at[near_rows].add(pair_exp)
        tile_weight = tile_exp / tile_rows(row_total)
        self_weight = self_exp / row_total
        pair_weight = pair_exp / row_total[near_rows]
        tile_wb = rounded(tile_weight)
        self_wb = rounded(self_weight)
        pair_wb = rounded(pair_weight)
        outcome = self_wb[:, :, None] * own_value
        outcome = outcome.at[flat_rows].add(jnp.einsum('shij,sjhe->sihe', tile_wb, tile_value).reshape(-1, HEADS, HEAD_DIM))
        outcome = outcome.at[near_rows].add(pair_wb[:, :, None] * far_value)
        row_delta = lax.optimization_barrier(jnp.sum(own_grad * outcome, axis=2))
        tile_drops = jnp.einsum('sihe,sjhe->shij', tile_grad, tile_value)
        tile_ds = rounded(tile_weight * (tile_drops - tile_rows(row_delta)))
        self_ds = rounded(self_weight * (lax.optimization_barrier(jnp.sum(own_grad * own_value, axis=2)) - row_delta))
        pair_ds = rounded(pair_weight * (lax.optimization_barrier(jnp.sum(near_grad * far_value, axis=2)) - row_delta[near_rows]))
        query_total = self_ds[:, :, None] * own_key
        query_total = query_total.at[flat_rows].add(jnp.einsum('shij,sjhe->sihe', tile_ds, tile_key).reshape(-1, HEADS, HEAD_DIM))
        query_total = query_total.at[near_rows].add(pair_ds[:, :, None] * far_key)
        empty_rows = jnp.zeros((group_size, HEADS, HEAD_DIM), jnp.float32)
        group_dk = empty_rows.at[flat_cols].add(jnp.einsum('shij,sihe->sjhe', tile_ds, tile_query).reshape(-1, HEADS, HEAD_DIM))
        group_dv = empty_rows.at[flat_cols].add(jnp.einsum('shij,sihe->sjhe', tile_wb, tile_grad).reshape(-1, HEADS, HEAD_DIM))
        group_dk = rounded(score_scale * group_dk).reshape(group_size, D)
        group_dv = rounded(group_dv).reshape(group_size, D)
        key_acc = lax.dynamic_update_slice_in_dim(key_acc, lax.dynamic_slice_in_dim(key_acc, group_start, group_size, 0) + group_dk, group_start, 0)
        value_acc = lax.dynamic_update_slice_in_dim(value_acc, lax.dynamic_slice_in_dim(value_acc, group_start, group_size, 0) + group_dv, group_start, 0)
        self_dk = (score_scale * self_ds[:, :, None] * own_query).reshape(NODE_DEV, D)
        self_dv = (self_wb[:, :, None] * own_grad).reshape(NODE_DEV, D)
        key_acc = lax.dynamic_update_slice_in_dim(key_acc, lax.dynamic_slice_in_dim(key_acc, own_start, NODE_DEV, 0) + self_dk, own_start, 0)
        value_acc = lax.dynamic_update_slice_in_dim(value_acc, lax.dynamic_slice_in_dim(value_acc, own_start, NODE_DEV, 0) + self_dv, own_start, 0)
        key_acc = key_acc.at[far_rows].add(rounded(score_scale * pair_ds[:, :, None] * near_query).reshape(-1, D))
        value_acc = value_acc.at[far_rows].add(rounded(pair_wb[:, :, None] * near_grad).reshape(-1, D))
        results = (outcome.reshape(NODE_DEV, D).astype(jnp.bfloat16), (score_scale * query_total).reshape(NODE_DEV, D).astype(jnp.bfloat16))
        return ((key_acc, value_acc), results)
    start_acc = jnp.zeros((NODES, D), jnp.float32)
    (key_acc, value_acc), (outcome, query_grad) = lax.scan(part_step, (start_acc, start_acc), jnp.arange(PARTS_SIZE, dtype=jnp.int32))
    return (outcome.reshape(NODES, D), query_grad.reshape(NODES, D), key_acc.astype(jnp.bfloat16), value_acc.astype(jnp.bfloat16))
```

```python
import functools
import math

import jax
import jax.numpy as jnp
from jax import lax
from jax.experimental import pallas as pl
from jax.experimental.pallas import tpu as pltpu
from jax.sharding import PartitionSpec as P

HEADS = 8
LANES = 128
VM = pl.BlockSpec(memory_space=pltpu.VMEM)
SM = pl.BlockSpec(memory_space=pltpu.SMEM)
ANY = pl.BlockSpec(memory_space=pl.ANY)
MESH = pl.DeviceIdType.MESH
F32 = jnp.float32
BF16 = jnp.bfloat16


def dot(a, b, dims):
    return lax.dot_general(a, b, (dims, ((), ())), preferred_element_type=F32)


NN = ((1,), (0,))
NT = ((1,), (1,))
TN = ((0,), (0,))


def pick_kernel(
    groups, domains, partner_ref, near_ref, key_ref, value_ref, out_ref, near_out, code_out
):
    matches, _, span = near_ref.shape
    rows = key_ref.shape[0]
    grp = lax.axis_index("grp")
    codes = [jnp.bitwise_xor(partner_ref[0, m] // domains, grp) for m in range(matches)]
    kinds = [
        jnp.where(c == groups // 2, 0, jnp.where(c > groups // 2, 1, 2)) for c in codes
    ]
    row_id = lax.broadcasted_iota(jnp.int32, (rows, span), 0)
    for m in range(matches):
        rank = jnp.int32(0)
        for o in range(matches):
            ahead = kinds[o] <= kinds[m] if o < m else kinds[o] < kinds[m]
            if o != m:
                rank = rank + ahead.astype(jnp.int32)
        near = near_ref[m, 0:1, :]
        near_out[pl.ds(rank, 1), :] = near
        code_out[pl.ds(rank, 1), :] = jnp.full((1, code_out.shape[1]), codes[m], jnp.int32)
        hot = (near == row_id).astype(BF16)
        at = pl.ds(pl.multiple_of(rank * span, span), span)
        out_ref[0, at, :] = dot(hot, key_ref[...], TN).astype(BF16)
        out_ref[1, at, :] = dot(hot, value_ref[...], TN).astype(BF16)


def flipped(me, bit):
    step = 1 << bit
    return me + step * (1 - 2 * ((me // step) % 2))


def comm_kernel(
    spread, n_top, groups, domains, matches, a_ref, b_ref, send_ref, code_ref,
    outa_ref, outb_ref, far_ref, recv, held, dsend, drecv, esend, erecv, lsem,
):
    dom = lax.axis_index("dom")
    grp = lax.axis_index("grp")
    rows = outa_ref.shape[0] // domains
    bits = groups.bit_length() - 1
    span = send_ref.shape[1] // matches
    barrier = pltpu.get_barrier_semaphore()
    for d in range(1, domains):
        pl.semaphore_signal(
            barrier, inc=1, device_id={"dom": lax.rem(dom + d, domains)}, device_id_type=MESH
        )
    for bit in range(bits):
        pl.semaphore_signal(
            barrier, inc=1, device_id={"grp": flipped(grp, bit)}, device_id_type=MESH
        )
    pl.semaphore_wait(barrier, domains - 1 + bits)

    def swap(stage, slot, src, dst):
        at = stage * matches + slot
        return pltpu.make_async_remote_copy(
            src_ref=src,
            dst_ref=dst,
            send_sem=esend.at[at],
            recv_sem=erecv.at[at],
            device_id={"grp": flipped(grp, bits - 1 - stage)},
            device_id_type=MESH,
        )

    def part(ref, slot):
        return ref.at[:, pl.ds(slot * span, span), :]

    moves = {}
    for slot in list(range(1, matches)) + [0]:
        first = 0 if slot < n_top else 1
        dst = part(far_ref, 0) if slot == 0 else part(recv.at[first], slot)
        moves[first, slot] = swap(first, slot, part(send_ref, slot), dst)
        moves[first, slot].start()
    mine = pl.ds(pl.multiple_of(dom * rows, rows), rows)
    locals_ = []
    spreads = []
    relay = spread and domains == 4
    near_x, near_y = flipped(dom, 0), flipped(dom, 1)

    def send_block(at, src, dst, owner, peer):
        there = pl.ds(pl.multiple_of(owner * rows, rows), rows)
        copy = pltpu.make_async_remote_copy(
            src_ref=src,
            dst_ref=dst.at[there, :],
            send_sem=dsend.at[at],
            recv_sem=drecv.at[at],
            device_id={"dom": peer},
            device_id_type=MESH,
        )
        copy.start()
        return copy

    if relay:
        a_x = send_block(0, a_ref, outa_ref, dom, near_x)
        b_y = send_block(1, b_ref, outb_ref, dom, near_y)
        b_x = send_block(2, b_ref, outb_ref, dom, near_x)
        a_y = send_block(3, a_ref, outa_ref, dom, near_y)
        spreads += [b_x, a_y]
    for which, (src, dst) in enumerate(((a_ref, outa_ref), (b_ref, outb_ref))):
        own = src if spread else src.at[mine, :]
        locals_.append(pltpu.make_async_copy(own, dst.at[mine, :], lsem.at[which]))
        locals_[-1].start()
        for d in range(1, domains) if not relay else ():
            peer = lax.rem(dom + d, domains)
            theirs = pl.ds(pl.multiple_of(peer * rows, rows), rows)
            copy = pltpu.make_async_remote_copy(
                src_ref=src if spread else src.at[theirs, :],
                dst_ref=dst.at[mine, :],
                send_sem=dsend.at[which * domains + d],
                recv_sem=drecv.at[which * domains + d],
                device_id={"dom": peer},
                device_id_type=MESH,
            )
            copy.start()
            spreads.append(copy)
    if relay:
        from_x = pl.ds(pl.multiple_of(near_x * rows, rows), rows)
        from_y = pl.ds(pl.multiple_of(near_y * rows, rows), rows)
        a_x.wait()
        spreads.append(send_block(4, outa_ref.at[from_x, :], outa_ref, near_x, near_y))
        b_y.wait()
        spreads.append(send_block(5, outb_ref.at[from_y, :], outb_ref, near_y, near_x))
    for stage in range(bits):
        last = stage == bits - 1
        others = list(range(n_top, matches)) if stage else []
        chosen = others + list(range(1, n_top))
        for slot in chosen:
            moves[stage, slot].wait_recv()
            piece = pl.ds(slot * span, span)
            fresh = stage == (0 if slot < n_top else 1)
            source = send_ref if fresh else held.at[stage - 1]
            taken = (code_ref[slot:slot + 1, :] // (1 << (bits - 1 - stage))) % 2 == 1
            target = far_ref if last else held.at[stage]
            for half in range(2):
                target[half, piece, :] = jnp.where(
                    taken, recv[stage, half, piece, :], source[half, piece, :]
                )
            if not last:
                moves[stage + 1, slot] = swap(
                    stage + 1, slot, part(held.at[stage], slot), part(recv.at[stage + 1], slot)
                )
                moves[stage + 1, slot].start()
    moves[0, 0].wait_recv()
    for move in moves.values():
        move.wait_send()
    for copy in spreads:
        copy.wait()
    for copy in locals_:
        copy.wait()


def comm(spread, cid, groups, domains, matches, n_top, a, b, send, code):
    rows = a.shape[0] if spread else a.shape[0] // domains
    width = a.shape[1]
    bits = groups.bit_length() - 1
    whole = jax.ShapeDtypeStruct((domains * rows, width), BF16)

    def call(tops):
        return pl.pallas_call(
            functools.partial(comm_kernel, spread, tops, groups, domains, matches),
            out_shape=(whole, whole, jax.ShapeDtypeStruct(send.shape, BF16)),
            in_specs=[VM, VM, VM, VM],
            out_specs=(ANY, ANY, VM),
            scratch_shapes=[
                pltpu.VMEM((bits,) + send.shape, BF16),
                pltpu.VMEM((max(bits - 1, 1),) + send.shape, BF16),
                pltpu.SemaphoreType.DMA((2 * domains,)),
                pltpu.SemaphoreType.DMA((2 * domains,)),
                pltpu.SemaphoreType.DMA((bits * matches,)),
                pltpu.SemaphoreType.DMA((bits * matches,)),
                pltpu.SemaphoreType.DMA((2,)),
            ],
            name=("gather_rows" if spread else "return_terms") + str(tops),
            compiler_params=pltpu.CompilerParams(
                collective_id=cid + tops - 1, has_side_effects=True
            ),
        )

    branches = [call(tops) for tops in range(1, matches + 1)]
    return lax.switch(n_top - 1, branches, a, b, send, code)


def attend_kernel(
    scale, entry_ref, count_ref, near_ref, q_ref, g_ref, gk_ref, gv_ref, far_ref, mask_ref,
    att_ref, gq_ref, kt_ref, vt_ref, back_ref, self_ref,
    table, masks, store, tops, sums, out_acc, q_acc, k_acc, v_acc,
):
    tile = mask_ref.shape[1]
    node_rows, width = q_ref.shape
    blocks = node_rows // tile
    edge_blocks = far_ref.shape[1] // tile
    group_blocks = gk_ref.shape[0] // tile
    slots = mask_ref.shape[0]
    pairs = width // LANES
    fixed = blocks + blocks * edge_blocks
    dom = lax.axis_index("dom")
    low = lax.broadcasted_iota(jnp.int32, (tile, LANES), 1) < (width // HEADS)
    row_id = lax.broadcasted_iota(jnp.int32, (tile, tile), 0)
    col_id = lax.broadcasted_iota(jnp.int32, (tile, tile), 1)
    zero = jnp.zeros((tile, LANES), BF16)

    def fill(t, a, kb, gb):
        table[t, 0] = a
        table[t, 1] = kb
        table[t, 2] = gb

    k_far = group_blocks + blocks
    for a in range(blocks):
        fill(a, a, dom * blocks + a, group_blocks + a)
        masks[a] = (row_id == col_id).astype(jnp.int32)
        for e in range(edge_blocks):
            t = blocks + a * edge_blocks + e
            fill(t, a, group_blocks + e, k_far + e)
            first = e * tile // near_ref.shape[1]
            last = (e + 1) * tile // near_ref.shape[1]
            near = jnp.concatenate([near_ref[r:r + 1, :] for r in range(first, last)], axis=1)
            masks[t] = (near == row_id + a * tile).astype(jnp.int32)
    for s in range(slots):
        live = s < count_ref[0]
        kb = jnp.where(live, entry_ref[1, 0, s] * blocks + entry_ref[2, 0, s], 0)
        fill(fixed + s, jnp.where(live, entry_ref[0, 0, s], 0), kb, kb)
        masks[fixed + s] = jnp.where(live, mask_ref[s], 0)
    assert (fixed + slots) % 2 == 0
    turns = (fixed + count_ref[0] + 1) // 2

    def each_tile(work):
        @pl.loop(0, turns)
        def _(i):
            for t in (2 * i, 2 * i + 1):
                work(t)

    @pl.loop(0, k_far + edge_blocks)
    def _(i):
        at = pl.ds(pl.multiple_of(i * tile, tile), tile)
        k_acc[at, :] = jnp.zeros((tile, width), F32)
        v_acc[at, :] = jnp.zeros((tile, width), F32)

    out_acc[...] = jnp.zeros_like(out_acc)
    q_acc[...] = jnp.zeros_like(q_acc)
    tops[...] = jnp.full_like(tops, -jnp.inf)
    sums[...] = jnp.zeros_like(sums)

    def cols(p):
        return slice(p * LANES, (p + 1) * LANES)

    def rows(i):
        return pl.ds(pl.multiple_of(i * tile, tile), tile)

    def split(x):
        return jnp.concatenate([jnp.where(low, x, zero), jnp.where(low, zero, x)], axis=0)

    def stack(y):
        return jnp.concatenate([y[:, :tile], y[:, tile:]], axis=0)

    def far_or_group(which, kb, p):
        ref = (gk_ref, gv_ref)[which]
        far_at = jnp.clip(kb - group_blocks, 0, edge_blocks - 1)
        near_at = jnp.minimum(kb, group_blocks - 1)
        return jnp.where(
            kb < group_blocks,
            ref[rows(near_at), cols(p)],
            far_ref[which, rows(far_at), cols(p)],
        )

    @each_tile
    def _(t):
        a = table[t, 0]
        kb = table[t, 1]
        live = masks[t] != 0
        live2 = jnp.concatenate([live, live], axis=1)
        for p in range(pairs):
            k2 = split(far_or_group(0, kb, p))
            s2 = dot(q_ref[rows(a), cols(p)], k2, NT) * scale
            s2 = jnp.where(live2, s2, -jnp.inf)
            store[t, p] = s2
            tops[a, p] = jnp.maximum(tops[a, p], s2)

    def spread_rows(x, reduce):
        left = jnp.broadcast_to(reduce(x[:, :tile], axis=1, keepdims=True), (tile, tile))
        right = jnp.broadcast_to(reduce(x[:, tile:], axis=1, keepdims=True), (tile, tile))
        return jnp.concatenate([left, right], axis=1)

    for i in range(blocks * pairs):
        a, p = i // pairs, i % pairs
        tops[a, p] = spread_rows(tops[a, p], jnp.max)

    @each_tile
    def _(t):
        a = table[t, 0]
        for p in range(pairs):
            e2 = jnp.exp(store[t, p] - tops[a, p])
            store[t, p] = e2
            sums[a, p] += e2

    for i in range(blocks * pairs):
        a, p = i // pairs, i % pairs
        sums[a, p] = 1.0 / spread_rows(sums[a, p], jnp.sum)

    @each_tile
    def _(t):
        a = table[t, 0]
        kb = table[t, 1]
        for p in range(pairs):
            w2 = store[t, p] * sums[a, p]
            store[t, p] = w2
            v2 = split(far_or_group(1, kb, p))
            out_acc[rows(a), cols(p)] += dot(w2.astype(BF16), v2, NN)

    att_ref[...] = out_acc[...].astype(BF16)
    for a in range(blocks):
        for p in range(pairs):
            at = slice(a * tile, (a + 1) * tile)
            prod = g_ref[at, cols(p)].astype(F32) * out_acc[at, cols(p)]
            left = jnp.sum(jnp.where(low, prod, 0.0), axis=1, keepdims=True)
            right = jnp.sum(jnp.where(low, 0.0, prod), axis=1, keepdims=True)
            tops[a, p] = jnp.concatenate(
                [jnp.broadcast_to(left, (tile, tile)), jnp.broadcast_to(right, (tile, tile))],
                axis=1,
            )

    @each_tile
    def _(t):
        a = table[t, 0]
        kb = table[t, 1]
        gb = table[t, 2]
        for p in range(pairs):
            w2 = store[t, p]
            k2 = split(far_or_group(0, kb, p))
            v2 = split(far_or_group(1, kb, p))
            q = q_ref[rows(a), cols(p)]
            g = g_ref[rows(a), cols(p)]
            drop = dot(g, v2, NT)
            ds = (w2 * (drop - tops[a, p])).astype(BF16)
            q_acc[rows(a), cols(p)] += dot(ds, k2, NN)
            k_acc[rows(gb), cols(p)] += dot(stack(ds), split(q), TN)
            v_acc[rows(gb), cols(p)] += dot(stack(w2.astype(BF16)), split(g), TN)

    gq_ref[...] = (scale * q_acc[...]).astype(BF16)

    @pl.loop(0, group_blocks)
    def _(i):
        kt_ref[rows(i), :] = (scale * k_acc[rows(i), :]).astype(BF16)
        vt_ref[rows(i), :] = v_acc[rows(i), :].astype(BF16)

    own = slice(group_blocks * tile, k_far * tile)
    far = slice(k_far * tile, (k_far + edge_blocks) * tile)
    self_ref[0] = scale * k_acc[own, :]
    self_ref[1] = v_acc[own, :]
    back_ref[0] = (scale * k_acc[far, :]).astype(BF16)
    back_ref[1] = v_acc[far, :].astype(BF16)


def finish_kernel(domains, near_ref, ka_ref, va_ref, back_ref, self_ref, gk_ref, gv_ref):
    rows = gk_ref.shape[0]
    matches = near_ref.shape[0]
    near = jnp.concatenate([near_ref[m:m + 1, :] for m in range(matches)], axis=1)
    hot = (near == lax.broadcasted_iota(jnp.int32, (rows, near.shape[1]), 0)).astype(BF16)
    for which, (src, dst) in enumerate(((ka_ref, gk_ref), (va_ref, gv_ref))):
        acc = self_ref[which] + dot(hot, back_ref[which], NN)
        for d in range(domains):
            acc = acc + src[d * rows:(d + 1) * rows, :].astype(F32)
        dst[...] = acc.astype(BF16)


def lanes_of(p):
    return pl.ds(pl.multiple_of(p * LANES, LANES), LANES)


def fused_kernel(
    n_top, scale, entry_ref, count_ref, partner_ref, near_ref,
    q_ref, k_ref, v_ref, g_ref, mask_ref,
    att_ref, gq_ref, gk_ref, gv_ref,
    keys, values, score, weight, bias, qs, q_t, g_t, hot, eye,
    tops, sums, delta, own_w, own_s, out_acc, q_acc,
    v_terms, k_terms, v_back, k_back,
    pick, far, recv, held, code_rows,
    edge_acc, edge_send, edge_recv, edge_held, edge_far,
    dsend, drecv, rsend, rrecv, esend, erecv, lsem,
):
    rows, width = q_ref.shape
    domains = keys.shape[0] - 1
    matches, _, span = near_ref.shape
    edges = matches * span
    tile = mask_ref.shape[1]
    slots = mask_ref.shape[0]
    blocks = rows // tile
    pairs = width // LANES
    half = width // HEADS
    groups = lax.axis_size("grp")
    bits = groups.bit_length() - 1
    dom = lax.axis_index("dom")
    grp = lax.axis_index("grp")
    near_x, near_y, across = flipped(dom, 0), flipped(dom, 1), flipped(flipped(dom, 0), 1)
    peers = (dom, near_x, near_y, across)
    edge_block = domains

    barrier = pltpu.get_barrier_semaphore()
    for d in range(1, domains):
        pl.semaphore_signal(barrier, inc=1, device_id={"dom": peers[d]}, device_id_type=MESH)
    for bit in range(bits):
        pl.semaphore_signal(
            barrier, inc=1, device_id={"grp": flipped(grp, bit)}, device_id_type=MESH
        )

    lane = lax.broadcasted_iota(jnp.int32, (rows, LANES), 1)
    low = lane < half
    row_id = lax.broadcasted_iota(jnp.int32, (rows, edges), 0)
    col_id = lax.broadcasted_iota(jnp.int32, (rows, edges), 1)
    eye[...] = (row_id == col_id).astype(BF16)

    codes = [jnp.bitwise_xor(partner_ref[0, m] // domains, grp) for m in range(matches)]
    kinds = [
        jnp.where(c == groups // 2, 0, jnp.where(c > groups // 2, 1, 2)) for c in codes
    ]
    ranks = []
    for m in range(matches):
        rank = jnp.int32(0)
        for o in range(matches):
            ahead = kinds[o] <= kinds[m] if o < m else kinds[o] < kinds[m]
            if o != m:
                rank = rank + ahead.astype(jnp.int32)
        ranks.append(rank)
    near_parts = []
    for r in range(matches):
        code = jnp.int32(0)
        ids = jnp.zeros((1, span), jnp.int32)
        for m in range(matches):
            here = (ranks[m] == r).astype(jnp.int32)
            code = code + here * codes[m]
            ids = ids + here * near_ref[m, 0:1, :]
        near_parts.append(ids)
        code_rows[r:r + 1, :] = jnp.full((1, width), code, jnp.int32)
    near = jnp.concatenate(near_parts, axis=1)
    hot_mask = near == row_id
    hot[...] = hot_mask.astype(BF16)
    bias[edge_block] = jnp.where(hot_mask, 0.0, -jnp.inf)

    pl.semaphore_wait(barrier, domains - 1 + bits)

    local_k = pltpu.make_async_copy(k_ref, keys.at[0], lsem.at[0])
    local_v = pltpu.make_async_copy(v_ref, values.at[0], lsem.at[1])

    def block(b):
        return pl.ds(b * tile, tile)

    def send(at, src, dst, peer):
        copy = pltpu.make_async_remote_copy(
            src_ref=src, dst_ref=dst, send_sem=dsend.at[at], recv_sem=drecv.at[at],
            device_id={"dom": peer}, device_id_type=MESH,
        )
        copy.start()
        return copy

    def spread(base, src, dst):
        x0 = send(base, src.at[block(0), :], dst.at[1, block(0), :], near_x)
        y1 = send(base + 1, src.at[block(1), :], dst.at[2, block(1), :], near_y)
        x1 = send(base + 2, src.at[block(1), :], dst.at[1, block(1), :], near_x)
        y0 = send(base + 3, src.at[block(0), :], dst.at[2, block(0), :], near_y)
        return [x0, y1, x1, y0]

    def relay(base, moves, dst):
        moves[0].wait_recv()
        first = send(base + 4, dst.at[1, block(0), :], dst.at[3, block(0), :], near_y)
        moves[1].wait_recv()
        second = send(base + 5, dst.at[2, block(1), :], dst.at[3, block(1), :], near_x)
        return moves + [first, second]

    k_moves = spread(0, k_ref, keys)
    local_k.start()
    local_v.start()

    def part(ref, slot):
        return ref.at[pl.ds(slot * span, span), :]

    def exchange(kind, src, recvs, helds, dst):
        def swap(stage, slot, source, target):
            at = stage * matches + slot
            return pltpu.make_async_remote_copy(
                src_ref=source, dst_ref=target,
                send_sem=esend.at[kind, at], recv_sem=erecv.at[kind, at],
                device_id={"grp": flipped(grp, bits - 1 - stage)}, device_id_type=MESH,
            )

        moves = {}

        def start():
            for slot in list(range(1, matches)) + [0]:
                first = 0 if slot < n_top else 1
                target = part(dst, 0) if slot == 0 else part(recvs.at[first], slot)
                moves[first, slot] = swap(first, slot, part(src, slot), target)
                moves[first, slot].start()

        def step(stage):
            last = stage == bits - 1
            others = list(range(n_top, matches)) if stage else []
            for slot in others + list(range(1, n_top)):
                moves[stage, slot].wait_recv()
                piece = pl.ds(slot * span, span)
                fresh = stage == (0 if slot < n_top else 1)
                source = src if fresh else helds.at[stage - 1]
                code = code_rows[slot:slot + 1, :dst.shape[1]]
                taken = (code // (1 << (bits - 1 - stage))) % 2 == 1
                target = dst if last else helds.at[stage]
                target[piece, :] = jnp.where(
                    taken, recvs[stage, piece, :], source[piece, :]
                )
                if not last:
                    moves[stage + 1, slot] = swap(
                        stage + 1, slot, part(helds.at[stage], slot),
                        part(recvs.at[stage + 1], slot),
                    )
                    moves[stage + 1, slot].start()
            if last:
                moves[0, 0].wait_recv()

        def drain():
            for move in moves.values():
                move.wait_send()

        return start, step, drain

    far_refs = (keys.at[edge_block], values.at[edge_block], far.at[0], far.at[1])
    swaps = [
        exchange(t, pick.at[t], recv.at[t], held.at[t], far_refs[t]) for t in range(4)
    ]

    hot_t = dot(eye[...], hot[...], NT).astype(BF16)
    for t, src in enumerate((k_ref, v_ref)):
        pick[t] = dot(hot_t, src[...], NN).astype(BF16)
        swaps[t][0]()

    qs[...] = (q_ref[...].astype(F32) * scale).astype(BF16)
    pick[2] = dot(hot_t, qs[...], NN).astype(BF16)
    pick[3] = dot(hot_t, g_ref[...], NN).astype(BF16)
    q_t[...] = jnp.transpose(qs[...].astype(F32)).astype(BF16)
    g_t[...] = jnp.transpose(g_ref[...].astype(F32)).astype(BF16)

    @pl.loop(0, domains * blocks * blocks)
    def _(i):
        j, a, b = i // (blocks * blocks), (i // blocks) % blocks, i % blocks
        c = (dom + j) % 2 + 2 * ((dom // 2 + j // 2) % 2)
        at, live = jnp.int32(0), jnp.int32(0)
        for s in range(slots):
            hit = (entry_ref[0, 0, s] == a) & (entry_ref[1, 0, s] == c)
            hit = (hit & (entry_ref[2, 0, s] == b) & (s < count_ref[0])).astype(jnp.int32)
            at = at + hit * s
            live = live + hit
        seen = mask_ref[at] * live
        ra = pl.ds(pl.multiple_of(a * tile, tile), tile)
        rb = pl.ds(pl.multiple_of(b * tile, tile), tile)
        bias[j, ra, rb] = jnp.where(seen != 0, 0.0, -jnp.inf)

    zero = jnp.zeros((rows, LANES), BF16)

    def split(x):
        return jnp.concatenate([jnp.where(low, x, zero), jnp.where(low, zero, x)], axis=0)

    def wide(x):
        left, right = x[:, :LANES], x[:, LANES:]
        return jnp.concatenate([left, left, right, right], axis=1)

    def fold(x, op):
        n = rows // LANES
        out = []
        for h in range(2):
            at = h * rows
            y = x[:, at:at + LANES]
            for i in range(1, n):
                y = op(y, x[:, at + i * LANES:at + (i + 1) * LANES])
            out.append(y)
        return jnp.concatenate(out, axis=1)

    def spread_rows(x, reduce):
        left = jnp.broadcast_to(reduce(x[:, :LANES], axis=1, keepdims=True), (rows, LANES))
        right = jnp.broadcast_to(reduce(x[:, LANES:], axis=1, keepdims=True), (rows, LANES))
        return jnp.concatenate([left, right], axis=1)

    def head_sums(x):
        left = jnp.sum(jnp.where(low, x, 0.0), axis=1, keepdims=True)
        right = jnp.sum(jnp.where(low, 0.0, x), axis=1, keepdims=True)
        return jnp.concatenate(
            [jnp.broadcast_to(left, (rows, LANES)), jnp.broadcast_to(right, (rows, LANES))],
            axis=1,
        )

    def by_lane(x):
        return jnp.where(low, x[:, :LANES], x[:, LANES:])

    def score_block(j):
        @pl.loop(0, pairs)
        def _(p):
            at = lanes_of(p)
            s = dot(qs[:, at], split(keys[j, :, at]), NT)
            b = bias[j]
            s = s + jnp.concatenate([b, b], axis=1)
            score[j, p] = s
            tops[p] = jnp.maximum(tops[p], fold(s, jnp.maximum))

    @pl.loop(0, pairs)
    def _(p):
        at = lanes_of(p)
        own = head_sums(qs[:, at].astype(F32) * k_ref[:, at].astype(F32))
        own_s[p] = own
        tops[p] = own
        sums[p] = jnp.zeros((rows, 2 * LANES), F32)
        out_acc[:, at] = jnp.zeros((rows, LANES), F32)
        q_acc[:, at] = jnp.zeros((rows, LANES), F32)

    local_k.wait()
    score_block(0)
    k_moves = relay(0, k_moves, keys)
    v_moves = spread(6, v_ref, values)
    k_moves[2].wait_recv()
    score_block(1)
    k_moves[3].wait_recv()
    score_block(2)
    swaps[0][1](0)
    k_moves[4].wait_recv()
    k_moves[5].wait_recv()
    score_block(3)
    v_moves = relay(6, v_moves, values)
    for stage in range(1, bits):
        swaps[0][1](stage)
    score_block(edge_block)

    @pl.loop(0, pairs)
    def _(p):
        tops[p] = spread_rows(tops[p], jnp.max)

    @pl.loop(0, (domains + 1) * pairs)
    def _(i):
        j, p = i // pairs, i % pairs
        e = jnp.exp(score[j, p] - wide(tops[p]))
        score[j, p] = e
        sums[p] += fold(e, jnp.add)

    @pl.loop(0, pairs)
    def _(p):
        e = jnp.exp(own_s[p] - tops[p])
        inv = 1.0 / (spread_rows(sums[p], jnp.sum) + e)
        sums[p] = inv
        own_w[p] = e * inv

    def back_copy(which, j, peer, src, dst):
        return pltpu.make_async_remote_copy(
            src_ref=src.at[j], dst_ref=dst.at[j],
            send_sem=rsend.at[which, j], recv_sem=rrecv.at[which, j],
            device_id={"dom": peer}, device_id_type=MESH,
        )

    def term(dst, j, p, left_t, x):
        for h in range(2):
            at = pl.ds(pl.multiple_of(p * LANES + h * half, half), half)
            y = dot(left_t[at, :], x[:, h * rows:(h + 1) * rows], NN)
            dst[j, at, :] = y.astype(BF16)

    def edge_rows(base, p, x):
        x = x.astype(F32)
        for h in range(2):
            y = jnp.sum(x[:, h * rows:(h + 1) * rows], axis=0, keepdims=True)
            edge_acc[pl.ds(base + 2 * p + h, 1), :] = y

    edge_acc[...] = jnp.zeros_like(edge_acc)

    def value_block(j):
        @pl.loop(0, pairs)
        def _(p):
            wb = (score[j, p] * wide(sums[p])).astype(BF16)
            weight[j, p] = wb
            term(v_terms, j, p, g_t, wb)

    v_copies = []
    for j in (3, 1, 2):
        value_block(j)
        v_copies.append(back_copy(0, j, peers[j], v_terms, v_back))
        v_copies[-1].start()
    swaps[1][1](0)
    value_block(0)

    @pl.loop(0, pairs)
    def _(p):
        wb = (score[edge_block, p] * wide(sums[p])).astype(BF16)
        weight[edge_block, p] = wb
        edge_rows(0, p, wb)

    for stage in range(1, bits):
        swaps[1][1](stage)
    for t in (2, 3):
        swaps[t][0]()
    local_v.wait()
    for move in v_moves[2:]:
        move.wait_recv()

    @pl.loop(0, (domains + 1) * pairs)
    def _(i):
        j, p = i // pairs, i % pairs
        at = lanes_of(p)
        out_acc[:, at] += dot(weight[j, p], split(values[j, :, at]), NN)

    @pl.loop(0, pairs)
    def _(p):
        at = lanes_of(p)
        own = own_w[p]
        wb = by_lane(own).astype(BF16).astype(F32)
        v, g = v_ref[:, at].astype(F32), g_ref[:, at].astype(F32)
        out = out_acc[:, at] + wb * v
        att_ref[:, at] = out.astype(BF16)
        d = head_sums(g * out)
        delta[p] = d
        own_s[p] = own * (head_sums(g * v) - d)

    def slope(j, p):
        at = lanes_of(p)
        drop = dot(g_ref[:, at], split(values[j, :, at]), NT)
        w = score[j, p] * wide(sums[p])
        ds = (w * (drop - wide(delta[p]))).astype(BF16)
        q_acc[:, at] += dot(ds, split(keys[j, :, at]), NN)
        return ds

    def key_block(j):
        @pl.loop(0, pairs)
        def _(p):
            term(k_terms, j, p, q_t, slope(j, p))

    k_copies = []
    for j in (3, 1, 2):
        key_block(j)
        k_copies.append(back_copy(1, j, peers[j], k_terms, k_back))
        k_copies[-1].start()

    @pl.loop(0, pairs)
    def _(p):
        edge_rows(HEADS, p, slope(edge_block, p))

    edge_send[...] = dot(eye[...], edge_acc[...].astype(BF16), NT).astype(BF16)
    edge_swap = exchange(4, edge_send, edge_recv, edge_held, edge_far)
    edge_swap[0]()
    key_block(0)

    @pl.loop(0, pairs)
    def _(p):
        at = lanes_of(p)
        ds = by_lane(own_s[p]).astype(BF16).astype(F32)
        wb = by_lane(own_w[p]).astype(BF16).astype(F32)
        gq_ref[:, at] = (
            scale * (q_acc[:, at] + ds * k_ref[:, at].astype(F32))
        ).astype(BF16)
        q_acc[:, at] = ds * qs[:, at].astype(F32)
        out_acc[:, at] = wb * g_ref[:, at].astype(F32)

    for stage in range(bits):
        edge_swap[1](stage)
    for t in (2, 3):
        for stage in range(bits):
            swaps[t][1](stage)

    col = lax.broadcasted_iota(jnp.int32, (LANES, width), 1) // half
    head = lax.broadcasted_iota(jnp.int32, (LANES, width), 0)
    for which, acc in ((0, out_acc), (1, q_acc)):
        grow = (head == col + which * HEADS).astype(BF16)
        piece = dot(edge_far[...], grow, NN) * far[1 - which].astype(F32)
        acc[...] += dot(hot[...], piece.astype(BF16), NN)

    for copy in v_copies:
        copy.wait_recv()
    for terms, back, acc, dst in (
        (v_terms, v_back, out_acc, gv_ref), (k_terms, k_back, q_acc, gk_ref)
    ):
        if dst is gk_ref:
            for copy in k_copies:
                copy.wait_recv()

        total = terms[0].astype(F32)
        for j in range(1, domains):
            total = total + back[j].astype(F32)
        dst[...] = (acc[...] + jnp.transpose(total)).astype(BF16)

    for copy in k_moves + v_moves + v_copies + k_copies:
        copy.wait_send()
    for swap in swaps + [edge_swap]:
        swap[2]()


def fused(
    n_top, groups, domains, matches, scale, query, key, value, cotangent,
    tile_index, tile_mask, tile_count, partner, near,
):
    rows, width = query.shape
    edges = matches * near.shape[2]
    pairs = width // LANES
    bits = groups.bit_length() - 1
    stats = pltpu.VMEM((pairs, rows, 2 * LANES), F32)
    wide = pltpu.VMEM((rows, width), F32)
    terms = pltpu.VMEM((domains, width, rows), BF16)
    DMA = pltpu.SemaphoreType.DMA

    def call(tops):
        return pl.pallas_call(
            functools.partial(fused_kernel, tops, scale),
            out_shape=(jax.ShapeDtypeStruct((rows, width), BF16),) * 4,
            in_specs=[SM, SM, SM] + [VM] * 6,
            out_specs=(VM,) * 4,
            scratch_shapes=[
                pltpu.VMEM((domains + 1, rows, width), BF16),
                pltpu.VMEM((domains + 1, rows, width), BF16),
                pltpu.VMEM((domains + 1, pairs, rows, 2 * rows), F32),
                pltpu.VMEM((domains + 1, pairs, rows, 2 * rows), BF16),
                pltpu.VMEM((domains + 1, rows, rows), F32),
                pltpu.VMEM((rows, width), BF16),
                pltpu.VMEM((width, rows), BF16),
                pltpu.VMEM((width, rows), BF16),
                pltpu.VMEM((rows, edges), BF16),
                pltpu.VMEM((rows, edges), BF16),
                stats, stats, stats, stats, stats,
                wide, wide,
                terms, terms, terms, terms,
                pltpu.VMEM((4, edges, width), BF16),
                pltpu.VMEM((2, edges, width), BF16),
                pltpu.VMEM((4, bits, edges, width), BF16),
                pltpu.VMEM((4, bits - 1, edges, width), BF16),
                pltpu.VMEM((matches, width), jnp.int32),
                pltpu.VMEM((LANES, edges), F32),
                pltpu.VMEM((edges, LANES), BF16),
                pltpu.VMEM((bits, edges, LANES), BF16),
                pltpu.VMEM((bits - 1, edges, LANES), BF16),
                pltpu.VMEM((edges, LANES), BF16),
                DMA((12,)), DMA((12,)),
                DMA((2, domains)), DMA((2, domains)),
                DMA((5, bits * matches)), DMA((5, bits * matches)),
                DMA((2,)),
            ],
            compiler_params=pltpu.CompilerParams(
                collective_id=tops - 1, has_side_effects=True, vmem_limit_bytes=60 << 20
            ),
            name="fused" + str(tops),
        )

    branches = [call(tops) for tops in range(1, matches + 1)]
    return lax.switch(
        n_top - 1, branches, tile_index, tile_count, partner, near,
        query, key, value, cotangent, tile_mask,
    )


def body(query, key, value, cotangent, tile_index, tile_mask, tile_count, partner, pair_edges):
    node_rows, width = query.shape
    head_size = width // HEADS
    scale = 1.0 / math.sqrt(head_size)
    domains = lax.axis_size("dom")
    groups = lax.axis_size("grp")
    matches, expander = pair_edges.shape[1], pair_edges.shape[2]
    edges = matches * expander
    tile = tile_mask.shape[2]
    slots = tile_mask.shape[1]
    blocks = node_rows // tile
    edge_blocks = edges // tile
    pairs = width // LANES
    codes = jnp.bitwise_xor(partner[0] // domains, lax.axis_index("grp"))
    n_top = jnp.sum((codes >= groups // 2).astype(jnp.int32))
    near_ids = jnp.transpose(pair_edges[0], (0, 2, 1))
    if domains == 4 and groups > 4 and blocks == 2 and edges == node_rows:
        return fused(
            n_top, groups, domains, matches, scale, query, key, value, cotangent,
            jnp.transpose(tile_index, (2, 0, 1)), tile_mask[0], tile_count, partner, near_ids,
        )
    pair_rows = jax.ShapeDtypeStruct((2, edges, width), BF16)
    send, near, code = pl.pallas_call(
        functools.partial(pick_kernel, groups, domains),
        out_shape=(
            pair_rows,
            jax.ShapeDtypeStruct((matches, expander), jnp.int32),
            jax.ShapeDtypeStruct((matches, width), jnp.int32),
        ),
        in_specs=[SM, VM, VM, VM],
        out_specs=(VM, VM, VM),
        name="pick_rows",
    )(partner, near_ids, key, value)
    group_key, group_value, far = comm(
        True, 0, groups, domains, matches, n_top, key, value, send, code
    )
    own_shape = jax.ShapeDtypeStruct((node_rows, width), BF16)
    group_blocks = domains * blocks
    tiles = slots + blocks + blocks * edge_blocks
    sources = (group_blocks + blocks + edge_blocks) * tile
    attended, grad_query, key_term, value_term, back, own_terms = pl.pallas_call(
        functools.partial(attend_kernel, scale),
        out_shape=(
            own_shape,
            own_shape,
            jax.ShapeDtypeStruct((domains * node_rows, width), BF16),
            jax.ShapeDtypeStruct((domains * node_rows, width), BF16),
            pair_rows,
            jax.ShapeDtypeStruct((2, node_rows, width), F32),
        ),
        in_specs=[SM, SM] + [VM] * 7,
        out_specs=(VM,) * 6,
        scratch_shapes=[
            pltpu.SMEM((tiles, 3), jnp.int32),
            pltpu.VMEM((tiles, tile, tile), jnp.int32),
            pltpu.VMEM((tiles, pairs, tile, 2 * tile), F32),
            pltpu.VMEM((blocks, pairs, tile, 2 * tile), F32),
            pltpu.VMEM((blocks, pairs, tile, 2 * tile), F32),
            pltpu.VMEM((node_rows, width), F32),
            pltpu.VMEM((node_rows, width), F32),
            pltpu.VMEM((sources, width), F32),
            pltpu.VMEM((sources, width), F32),
        ],
        compiler_params=pltpu.CompilerParams(vmem_limit_bytes=60 << 20),
        name="attend",
    )(
        jnp.transpose(tile_index, (2, 0, 1)), tile_count, near, query, cotangent,
        group_key, group_value, far, tile_mask[0],
    )
    key_parts, value_parts, returned = comm(
        False, matches, groups, domains, matches, n_top, key_term, value_term, back, code
    )
    grad_key, grad_value = pl.pallas_call(
        functools.partial(finish_kernel, domains),
        out_shape=(own_shape, own_shape),
        in_specs=[VM] * 5,
        out_specs=(VM, VM),
        name="finish",
    )(near, key_parts, value_parts, returned, own_terms)
    return attended, grad_query, grad_key, grad_value


def solution(mesh):
    nodes = P(("grp", "dom"), None)
    return jax.shard_map(
        body,
        mesh=mesh,
        in_specs=(
            nodes, nodes, nodes, nodes,
            P(("grp", "dom"), None, None),
            P(("grp", "dom"), None, None, None),
            P(("grp", "dom")),
            nodes,
            P(("grp", "dom"), None, None, None),
        ),
        out_specs=(nodes, nodes, nodes, nodes),
        check_vma=False,
    )
```

```python
import functools
import math

import jax
import jax.numpy as jnp
from jax import lax
from jax.experimental import pallas as pl
from jax.experimental.pallas import tpu as pltpu
from jax.sharding import PartitionSpec as P

HEADS = 8
LANES = 128
VM = pl.BlockSpec(memory_space=pltpu.VMEM)
SM = pl.BlockSpec(memory_space=pltpu.SMEM)
ANY = pl.BlockSpec(memory_space=pl.ANY)
MESH = pl.DeviceIdType.MESH
F32 = jnp.float32
BF16 = jnp.bfloat16


def dot(a, b, dims):
    return lax.dot_general(a, b, (dims, ((), ())), preferred_element_type=F32)


NN = ((1,), (0,))
NT = ((1,), (1,))
TN = ((0,), (0,))


def pick_kernel(
    groups, domains, partner_ref, near_ref, key_ref, value_ref, out_ref, near_out, code_out
):
    matches, _, span = near_ref.shape
    rows = key_ref.shape[0]
    grp = lax.axis_index("grp")
    codes = [jnp.bitwise_xor(partner_ref[0, m] // domains, grp) for m in range(matches)]
    kinds = [
        jnp.where(c == groups // 2, 0, jnp.where(c > groups // 2, 1, 2)) for c in codes
    ]
    row_id = lax.broadcasted_iota(jnp.int32, (rows, span), 0)
    for m in range(matches):
        rank = jnp.int32(0)
        for o in range(matches):
            ahead = kinds[o] <= kinds[m] if o < m else kinds[o] < kinds[m]
            if o != m:
                rank = rank + ahead.astype(jnp.int32)
        near = near_ref[m, 0:1, :]
        near_out[pl.ds(rank, 1), :] = near
        code_out[pl.ds(rank, 1), :] = jnp.full((1, code_out.shape[1]), codes[m], jnp.int32)
        hot = (near == row_id).astype(BF16)
        at = pl.ds(pl.multiple_of(rank * span, span), span)
        out_ref[0, at, :] = dot(hot, key_ref[...], TN).astype(BF16)
        out_ref[1, at, :] = dot(hot, value_ref[...], TN).astype(BF16)


def flipped(me, bit):
    step = 1 << bit
    return me + step * (1 - 2 * ((me // step) % 2))


def comm_kernel(
    spread, n_top, groups, domains, matches, a_ref, b_ref, send_ref, code_ref,
    outa_ref, outb_ref, far_ref, recv, held, dsend, drecv, esend, erecv, lsem,
):
    dom = lax.axis_index("dom")
    grp = lax.axis_index("grp")
    rows = outa_ref.shape[0] // domains
    bits = groups.bit_length() - 1
    span = send_ref.shape[1] // matches
    barrier = pltpu.get_barrier_semaphore()
    for d in range(1, domains):
        pl.semaphore_signal(
            barrier, inc=1, device_id={"dom": lax.rem(dom + d, domains)}, device_id_type=MESH
        )
    for bit in range(bits):
        pl.semaphore_signal(
            barrier, inc=1, device_id={"grp": flipped(grp, bit)}, device_id_type=MESH
        )
    pl.semaphore_wait(barrier, domains - 1 + bits)

    def swap(stage, slot, src, dst):
        at = stage * matches + slot
        return pltpu.make_async_remote_copy(
            src_ref=src,
            dst_ref=dst,
            send_sem=esend.at[at],
            recv_sem=erecv.at[at],
            device_id={"grp": flipped(grp, bits - 1 - stage)},
            device_id_type=MESH,
        )

    def part(ref, slot):
        return ref.at[:, pl.ds(slot * span, span), :]

    moves = {}
    for slot in list(range(1, matches)) + [0]:
        first = 0 if slot < n_top else 1
        dst = part(far_ref, 0) if slot == 0 else part(recv.at[first], slot)
        moves[first, slot] = swap(first, slot, part(send_ref, slot), dst)
        moves[first, slot].start()
    mine = pl.ds(pl.multiple_of(dom * rows, rows), rows)
    locals_ = []
    spreads = []
    relay = spread and domains == 4
    near_x, near_y = flipped(dom, 0), flipped(dom, 1)

    def send_block(at, src, dst, owner, peer):
        there = pl.ds(pl.multiple_of(owner * rows, rows), rows)
        copy = pltpu.make_async_remote_copy(
            src_ref=src,
            dst_ref=dst.at[there, :],
            send_sem=dsend.at[at],
            recv_sem=drecv.at[at],
            device_id={"dom": peer},
            device_id_type=MESH,
        )
        copy.start()
        return copy

    if relay:
        a_x = send_block(0, a_ref, outa_ref, dom, near_x)
        b_y = send_block(1, b_ref, outb_ref, dom, near_y)
        b_x = send_block(2, b_ref, outb_ref, dom, near_x)
        a_y = send_block(3, a_ref, outa_ref, dom, near_y)
        spreads += [b_x, a_y]
    for which, (src, dst) in enumerate(((a_ref, outa_ref), (b_ref, outb_ref))):
        own = src if spread else src.at[mine, :]
        locals_.append(pltpu.make_async_copy(own, dst.at[mine, :], lsem.at[which]))
        locals_[-1].start()
        for d in range(1, domains) if not relay else ():
            peer = lax.rem(dom + d, domains)
            theirs = pl.ds(pl.multiple_of(peer * rows, rows), rows)
            copy = pltpu.make_async_remote_copy(
                src_ref=src if spread else src.at[theirs, :],
                dst_ref=dst.at[mine, :],
                send_sem=dsend.at[which * domains + d],
                recv_sem=drecv.at[which * domains + d],
                device_id={"dom": peer},
                device_id_type=MESH,
            )
            copy.start()
            spreads.append(copy)
    if relay:
        from_x = pl.ds(pl.multiple_of(near_x * rows, rows), rows)
        from_y = pl.ds(pl.multiple_of(near_y * rows, rows), rows)
        a_x.wait()
        spreads.append(send_block(4, outa_ref.at[from_x, :], outa_ref, near_x, near_y))
        b_y.wait()
        spreads.append(send_block(5, outb_ref.at[from_y, :], outb_ref, near_y, near_x))
    for stage in range(bits):
        last = stage == bits - 1
        others = list(range(n_top, matches)) if stage else []
        chosen = others + list(range(1, n_top))
        for slot in chosen:
            moves[stage, slot].wait_recv()
            piece = pl.ds(slot * span, span)
            fresh = stage == (0 if slot < n_top else 1)
            source = send_ref if fresh else held.at[stage - 1]
            taken = (code_ref[slot:slot + 1, :] // (1 << (bits - 1 - stage))) % 2 == 1
            target = far_ref if last else held.at[stage]
            for half in range(2):
                target[half, piece, :] = jnp.where(
                    taken, recv[stage, half, piece, :], source[half, piece, :]
                )
            if not last:
                moves[stage + 1, slot] = swap(
                    stage + 1, slot, part(held.at[stage], slot), part(recv.at[stage + 1], slot)
                )
                moves[stage + 1, slot].start()
    moves[0, 0].wait_recv()
    for move in moves.values():
        move.wait_send()
    for copy in spreads:
        copy.wait()
    for copy in locals_:
        copy.wait()


def comm(spread, cid, groups, domains, matches, n_top, a, b, send, code):
    rows = a.shape[0] if spread else a.shape[0] // domains
    width = a.shape[1]
    bits = groups.bit_length() - 1
    whole = jax.ShapeDtypeStruct((domains * rows, width), BF16)

    def call(tops):
        return pl.pallas_call(
            functools.partial(comm_kernel, spread, tops, groups, domains, matches),
            out_shape=(whole, whole, jax.ShapeDtypeStruct(send.shape, BF16)),
            in_specs=[VM, VM, VM, VM],
            out_specs=(ANY, ANY, VM),
            scratch_shapes=[
                pltpu.VMEM((bits,) + send.shape, BF16),
                pltpu.VMEM((max(bits - 1, 1),) + send.shape, BF16),
                pltpu.SemaphoreType.DMA((2 * domains,)),
                pltpu.SemaphoreType.DMA((2 * domains,)),
                pltpu.SemaphoreType.DMA((bits * matches,)),
                pltpu.SemaphoreType.DMA((bits * matches,)),
                pltpu.SemaphoreType.DMA((2,)),
            ],
            name=("gather_rows" if spread else "return_terms") + str(tops),
            compiler_params=pltpu.CompilerParams(
                collective_id=cid + tops - 1, has_side_effects=True
            ),
        )

    branches = [call(tops) for tops in range(1, matches + 1)]
    return lax.switch(n_top - 1, branches, a, b, send, code)


def attend_kernel(
    scale, entry_ref, count_ref, near_ref, q_ref, g_ref, gk_ref, gv_ref, far_ref, mask_ref,
    att_ref, gq_ref, kt_ref, vt_ref, back_ref, self_ref,
    table, masks, store, tops, sums, out_acc, q_acc, k_acc, v_acc,
):
    tile = mask_ref.shape[1]
    node_rows, width = q_ref.shape
    blocks = node_rows // tile
    edge_blocks = far_ref.shape[1] // tile
    group_blocks = gk_ref.shape[0] // tile
    slots = mask_ref.shape[0]
    pairs = width // LANES
    fixed = blocks + blocks * edge_blocks
    dom = lax.axis_index("dom")
    low = lax.broadcasted_iota(jnp.int32, (tile, LANES), 1) < (width // HEADS)
    row_id = lax.broadcasted_iota(jnp.int32, (tile, tile), 0)
    col_id = lax.broadcasted_iota(jnp.int32, (tile, tile), 1)
    zero = jnp.zeros((tile, LANES), BF16)

    def fill(t, a, kb, gb):
        table[t, 0] = a
        table[t, 1] = kb
        table[t, 2] = gb

    k_far = group_blocks + blocks
    for a in range(blocks):
        fill(a, a, dom * blocks + a, group_blocks + a)
        masks[a] = (row_id == col_id).astype(jnp.int32)
        for e in range(edge_blocks):
            t = blocks + a * edge_blocks + e
            fill(t, a, group_blocks + e, k_far + e)
            first = e * tile // near_ref.shape[1]
            last = (e + 1) * tile // near_ref.shape[1]
            near = jnp.concatenate([near_ref[r:r + 1, :] for r in range(first, last)], axis=1)
            masks[t] = (near == row_id + a * tile).astype(jnp.int32)
    for s in range(slots):
        live = s < count_ref[0]
        kb = jnp.where(live, entry_ref[1, 0, s] * blocks + entry_ref[2, 0, s], 0)
        fill(fixed + s, jnp.where(live, entry_ref[0, 0, s], 0), kb, kb)
        masks[fixed + s] = jnp.where(live, mask_ref[s], 0)
    assert (fixed + slots) % 2 == 0
    turns = (fixed + count_ref[0] + 1) // 2

    def each_tile(work):
        @pl.loop(0, turns)
        def _(i):
            for t in (2 * i, 2 * i + 1):
                work(t)

    @pl.loop(0, k_far + edge_blocks)
    def _(i):
        at = pl.ds(pl.multiple_of(i * tile, tile), tile)
        k_acc[at, :] = jnp.zeros((tile, width), F32)
        v_acc[at, :] = jnp.zeros((tile, width), F32)

    out_acc[...] = jnp.zeros_like(out_acc)
    q_acc[...] = jnp.zeros_like(q_acc)
    tops[...] = jnp.full_like(tops, -jnp.inf)
    sums[...] = jnp.zeros_like(sums)

    def cols(p):
        return slice(p * LANES, (p + 1) * LANES)

    def rows(i):
        return pl.ds(pl.multiple_of(i * tile, tile), tile)

    def split(x):
        return jnp.concatenate([jnp.where(low, x, zero), jnp.where(low, zero, x)], axis=0)

    def stack(y):
        return jnp.concatenate([y[:, :tile], y[:, tile:]], axis=0)

    def far_or_group(which, kb, p):
        ref = (gk_ref, gv_ref)[which]
        far_at = jnp.clip(kb - group_blocks, 0, edge_blocks - 1)
        near_at = jnp.minimum(kb, group_blocks - 1)
        return jnp.where(
            kb < group_blocks,
            ref[rows(near_at), cols(p)],
            far_ref[which, rows(far_at), cols(p)],
        )

    @each_tile
    def _(t):
        a = table[t, 0]
        kb = table[t, 1]
        live = masks[t] != 0
        live2 = jnp.concatenate([live, live], axis=1)
        for p in range(pairs):
            k2 = split(far_or_group(0, kb, p))
            s2 = dot(q_ref[rows(a), cols(p)], k2, NT) * scale
            s2 = jnp.where(live2, s2, -jnp.inf)
            store[t, p] = s2
            tops[a, p] = jnp.maximum(tops[a, p], s2)

    def spread_rows(x, reduce):
        left = jnp.broadcast_to(reduce(x[:, :tile], axis=1, keepdims=True), (tile, tile))
        right = jnp.broadcast_to(reduce(x[:, tile:], axis=1, keepdims=True), (tile, tile))
        return jnp.concatenate([left, right], axis=1)

    for i in range(blocks * pairs):
        a, p = i // pairs, i % pairs
        tops[a, p] = spread_rows(tops[a, p], jnp.max)

    @each_tile
    def _(t):
        a = table[t, 0]
        for p in range(pairs):
            e2 = jnp.exp(store[t, p] - tops[a, p])
            store[t, p] = e2
            sums[a, p] += e2

    for i in range(blocks * pairs):
        a, p = i // pairs, i % pairs
        sums[a, p] = 1.0 / spread_rows(sums[a, p], jnp.sum)

    @each_tile
    def _(t):
        a = table[t, 0]
        kb = table[t, 1]
        for p in range(pairs):
            w2 = store[t, p] * sums[a, p]
            store[t, p] = w2
            v2 = split(far_or_group(1, kb, p))
            out_acc[rows(a), cols(p)] += dot(w2.astype(BF16), v2, NN)

    att_ref[...] = out_acc[...].astype(BF16)
    for a in range(blocks):
        for p in range(pairs):
            at = slice(a * tile, (a + 1) * tile)
            prod = g_ref[at, cols(p)].astype(F32) * out_acc[at, cols(p)]
            left = jnp.sum(jnp.where(low, prod, 0.0), axis=1, keepdims=True)
            right = jnp.sum(jnp.where(low, 0.0, prod), axis=1, keepdims=True)
            tops[a, p] = jnp.concatenate(
                [jnp.broadcast_to(left, (tile, tile)), jnp.broadcast_to(right, (tile, tile))],
                axis=1,
            )

    @each_tile
    def _(t):
        a = table[t, 0]
        kb = table[t, 1]
        gb = table[t, 2]
        for p in range(pairs):
            w2 = store[t, p]
            k2 = split(far_or_group(0, kb, p))
            v2 = split(far_or_group(1, kb, p))
            q = q_ref[rows(a), cols(p)]
            g = g_ref[rows(a), cols(p)]
            drop = dot(g, v2, NT)
            ds = (w2 * (drop - tops[a, p])).astype(BF16)
            q_acc[rows(a), cols(p)] += dot(ds, k2, NN)
            k_acc[rows(gb), cols(p)] += dot(stack(ds), split(q), TN)
            v_acc[rows(gb), cols(p)] += dot(stack(w2.astype(BF16)), split(g), TN)

    gq_ref[...] = (scale * q_acc[...]).astype(BF16)

    @pl.loop(0, group_blocks)
    def _(i):
        kt_ref[rows(i), :] = (scale * k_acc[rows(i), :]).astype(BF16)
        vt_ref[rows(i), :] = v_acc[rows(i), :].astype(BF16)

    own = slice(group_blocks * tile, k_far * tile)
    far = slice(k_far * tile, (k_far + edge_blocks) * tile)
    self_ref[0] = scale * k_acc[own, :]
    self_ref[1] = v_acc[own, :]
    back_ref[0] = (scale * k_acc[far, :]).astype(BF16)
    back_ref[1] = v_acc[far, :].astype(BF16)


def finish_kernel(domains, near_ref, ka_ref, va_ref, back_ref, self_ref, gk_ref, gv_ref):
    rows = gk_ref.shape[0]
    matches = near_ref.shape[0]
    near = jnp.concatenate([near_ref[m:m + 1, :] for m in range(matches)], axis=1)
    hot = (near == lax.broadcasted_iota(jnp.int32, (rows, near.shape[1]), 0)).astype(BF16)
    for which, (src, dst) in enumerate(((ka_ref, gk_ref), (va_ref, gv_ref))):
        acc = self_ref[which] + dot(hot, back_ref[which], NN)
        for d in range(domains):
            acc = acc + src[d * rows:(d + 1) * rows, :].astype(F32)
        dst[...] = acc.astype(BF16)


def lanes_of(p):
    return pl.ds(pl.multiple_of(p * LANES, LANES), LANES)


def fused_kernel(
    n_top, scale, entry_ref, count_ref, partner_ref, near_ref,
    q_ref, k_ref, v_ref, g_ref, mask_ref,
    att_ref, gq_ref, gk_ref, gv_ref,
    keys, values, score, weight, bias, qs, q_t, g_t, hot, eye,
    tops, sums, delta, own_w, own_s, out_acc, q_acc,
    v_terms, k_terms, v_back, k_back,
    pick, far, recv, held, code_rows,
    edge_acc, edge_send, edge_recv, edge_held, edge_far,
    dsend, drecv, rsend, rrecv, esend, erecv, lsem,
):
    rows, width = q_ref.shape
    domains = keys.shape[0] - 1
    matches, _, span = near_ref.shape
    edges = matches * span
    tile = mask_ref.shape[1]
    slots = mask_ref.shape[0]
    blocks = rows // tile
    pairs = width // LANES
    half = width // HEADS
    groups = lax.axis_size("grp")
    bits = groups.bit_length() - 1
    dom = lax.axis_index("dom")
    grp = lax.axis_index("grp")
    near_x, near_y, across = flipped(dom, 0), flipped(dom, 1), flipped(flipped(dom, 0), 1)
    peers = (dom, near_x, near_y, across)
    edge_block = domains

    barrier = pltpu.get_barrier_semaphore()
    for d in range(1, domains):
        pl.semaphore_signal(barrier, inc=1, device_id={"dom": peers[d]}, device_id_type=MESH)
    for bit in range(bits):
        pl.semaphore_signal(
            barrier, inc=1, device_id={"grp": flipped(grp, bit)}, device_id_type=MESH
        )

    lane = lax.broadcasted_iota(jnp.int32, (rows, LANES), 1)
    low = lane < half
    row_id = lax.broadcasted_iota(jnp.int32, (rows, edges), 0)
    col_id = lax.broadcasted_iota(jnp.int32, (rows, edges), 1)
    eye[...] = (row_id == col_id).astype(BF16)

    local_k = pltpu.make_async_copy(k_ref, keys.at[0], lsem.at[0])
    local_v = pltpu.make_async_copy(v_ref, values.at[0], lsem.at[1])

    def block(b):
        return pl.ds(b * tile, tile)

    def send(at, src, dst, peer):
        copy = pltpu.make_async_remote_copy(
            src_ref=src, dst_ref=dst, send_sem=dsend.at[at], recv_sem=drecv.at[at],
            device_id={"dom": peer}, device_id_type=MESH,
        )
        copy.start()
        return copy

    def spread(base, src, dst):
        x0 = send(base, src.at[block(0), :], dst.at[1, block(0), :], near_x)
        y1 = send(base + 1, src.at[block(1), :], dst.at[2, block(1), :], near_y)
        x1 = send(base + 2, src.at[block(1), :], dst.at[1, block(1), :], near_x)
        y0 = send(base + 3, src.at[block(0), :], dst.at[2, block(0), :], near_y)
        return [x0, y1, x1, y0]

    def relay(base, moves, dst):
        moves[0].wait_recv()
        first = send(base + 4, dst.at[1, block(0), :], dst.at[3, block(0), :], near_y)
        moves[1].wait_recv()
        second = send(base + 5, dst.at[2, block(1), :], dst.at[3, block(1), :], near_x)
        return moves + [first, second]

    pl.semaphore_wait(barrier, domains - 1 + bits)
    k_moves = spread(0, k_ref, keys)
    local_k.start()
    local_v.start()

    codes = [jnp.bitwise_xor(partner_ref[0, m] // domains, grp) for m in range(matches)]
    kinds = [
        jnp.where(c == groups // 2, 0, jnp.where(c > groups // 2, 1, 2)) for c in codes
    ]
    ranks = []
    for m in range(matches):
        rank = jnp.int32(0)
        for o in range(matches):
            ahead = kinds[o] <= kinds[m] if o < m else kinds[o] < kinds[m]
            if o != m:
                rank = rank + ahead.astype(jnp.int32)
        ranks.append(rank)
    near_parts = []
    for r in range(matches):
        code = jnp.int32(0)
        ids = jnp.zeros((1, span), jnp.int32)
        for m in range(matches):
            here = (ranks[m] == r).astype(jnp.int32)
            code = code + here * codes[m]
            ids = ids + here * near_ref[m, 0:1, :]
        near_parts.append(ids)
        code_rows[r:r + 1, :] = jnp.full((1, width), code, jnp.int32)
    near = jnp.concatenate(near_parts, axis=1)
    hot_mask = near == row_id
    hot[...] = hot_mask.astype(BF16)
    bias[edge_block] = jnp.where(hot_mask, 0.0, -jnp.inf)

    def part(ref, slot):
        return ref.at[pl.ds(slot * span, span), :]

    def exchange(kind, src, recvs, helds, dst):
        def swap(stage, slot, source, target):
            at = stage * matches + slot
            return pltpu.make_async_remote_copy(
                src_ref=source, dst_ref=target,
                send_sem=esend.at[kind, at], recv_sem=erecv.at[kind, at],
                device_id={"grp": flipped(grp, bits - 1 - stage)}, device_id_type=MESH,
            )

        moves = {}

        def start():
            for slot in list(range(1, matches)) + [0]:
                first = 0 if slot < n_top else 1
                target = part(dst, 0) if slot == 0 else part(recvs.at[first], slot)
                moves[first, slot] = swap(first, slot, part(src, slot), target)
                moves[first, slot].start()

        def step(stage):
            last = stage == bits - 1
            others = list(range(n_top, matches)) if stage else []
            for slot in others + list(range(1, n_top)):
                moves[stage, slot].wait_recv()
                piece = pl.ds(slot * span, span)
                fresh = stage == (0 if slot < n_top else 1)
                source = src if fresh else helds.at[stage - 1]
                code = code_rows[slot:slot + 1, :dst.shape[1]]
                taken = (code // (1 << (bits - 1 - stage))) % 2 == 1
                target = dst if last else helds.at[stage]
                target[piece, :] = jnp.where(
                    taken, recvs[stage, piece, :], source[piece, :]
                )
                if not last:
                    moves[stage + 1, slot] = swap(
                        stage + 1, slot, part(helds.at[stage], slot),
                        part(recvs.at[stage + 1], slot),
                    )
                    moves[stage + 1, slot].start()
            if last:
                moves[0, 0].wait_recv()

        def drain():
            for move in moves.values():
                move.wait_send()

        return start, step, drain

    far_refs = (keys.at[edge_block], values.at[edge_block], far.at[0], far.at[1])
    swaps = [
        exchange(t, pick.at[t], recv.at[t], held.at[t], far_refs[t]) for t in range(4)
    ]

    hot_t = dot(eye[...], hot[...], NT).astype(BF16)
    for t, src in enumerate((k_ref, v_ref)):
        pick[t] = dot(hot_t, src[...], NN).astype(BF16)
        swaps[t][0]()

    qs[...] = (q_ref[...].astype(F32) * scale).astype(BF16)
    pick[2] = dot(hot_t, qs[...], NN).astype(BF16)
    pick[3] = dot(hot_t, g_ref[...], NN).astype(BF16)
    k_moves = relay(0, k_moves, keys)
    v_moves = spread(6, v_ref, values)
    q_t[...] = jnp.transpose(qs[...].astype(F32)).astype(BF16)
    g_t[...] = jnp.transpose(g_ref[...].astype(F32)).astype(BF16)

    @pl.loop(0, domains * blocks * blocks)
    def _(i):
        j, a, b = i // (blocks * blocks), (i // blocks) % blocks, i % blocks
        c = (dom + j) % 2 + 2 * ((dom // 2 + j // 2) % 2)
        at, live = jnp.int32(0), jnp.int32(0)
        for s in range(slots):
            hit = (entry_ref[0, 0, s] == a) & (entry_ref[1, 0, s] == c)
            hit = (hit & (entry_ref[2, 0, s] == b) & (s < count_ref[0])).astype(jnp.int32)
            at = at + hit * s
            live = live + hit
        seen = mask_ref[at] * live
        ra = pl.ds(pl.multiple_of(a * tile, tile), tile)
        rb = pl.ds(pl.multiple_of(b * tile, tile), tile)
        bias[j, ra, rb] = jnp.where(seen != 0, 0.0, -jnp.inf)

    zero = jnp.zeros((rows, LANES), BF16)

    def split(x):
        return jnp.concatenate([jnp.where(low, x, zero), jnp.where(low, zero, x)], axis=0)

    def wide(x):
        left, right = x[:, :LANES], x[:, LANES:]
        return jnp.concatenate([left, left, right, right], axis=1)

    def fold(x, op):
        n = rows // LANES
        out = []
        for h in range(2):
            at = h * rows
            y = x[:, at:at + LANES]
            for i in range(1, n):
                y = op(y, x[:, at + i * LANES:at + (i + 1) * LANES])
            out.append(y)
        return jnp.concatenate(out, axis=1)

    def spread_rows(x, reduce):
        left = jnp.broadcast_to(reduce(x[:, :LANES], axis=1, keepdims=True), (rows, LANES))
        right = jnp.broadcast_to(reduce(x[:, LANES:], axis=1, keepdims=True), (rows, LANES))
        return jnp.concatenate([left, right], axis=1)

    def head_sums(x):
        left = jnp.sum(jnp.where(low, x, 0.0), axis=1, keepdims=True)
        right = jnp.sum(jnp.where(low, 0.0, x), axis=1, keepdims=True)
        return jnp.concatenate(
            [jnp.broadcast_to(left, (rows, LANES)), jnp.broadcast_to(right, (rows, LANES))],
            axis=1,
        )

    def by_lane(x):
        return jnp.where(low, x[:, :LANES], x[:, LANES:])

    def score_block(j):
        @pl.loop(0, pairs)
        def _(p):
            at = lanes_of(p)
            s = dot(qs[:, at], split(keys[j, :, at]), NT)
            b = bias[j]
            s = s + jnp.concatenate([b, b], axis=1)
            score[j, p] = s
            tops[p] = jnp.maximum(tops[p], fold(s, jnp.maximum))

    @pl.loop(0, pairs)
    def _(p):
        at = lanes_of(p)
        own = head_sums(qs[:, at].astype(F32) * k_ref[:, at].astype(F32))
        own_s[p] = own
        tops[p] = own
        sums[p] = jnp.zeros((rows, 2 * LANES), F32)
        out_acc[:, at] = jnp.zeros((rows, LANES), F32)
        q_acc[:, at] = jnp.zeros((rows, LANES), F32)

    local_k.wait()
    score_block(0)
    k_moves[2].wait_recv()
    score_block(1)
    k_moves[3].wait_recv()
    score_block(2)
    swaps[0][1](0)
    k_moves[4].wait_recv()
    k_moves[5].wait_recv()
    score_block(3)
    v_moves = relay(6, v_moves, values)
    for stage in range(1, bits):
        swaps[0][1](stage)
    score_block(edge_block)

    @pl.loop(0, pairs)
    def _(p):
        tops[p] = spread_rows(tops[p], jnp.max)

    @pl.loop(0, (domains + 1) * pairs)
    def _(i):
        j, p = i // pairs, i % pairs
        e = jnp.exp(score[j, p] - wide(tops[p]))
        score[j, p] = e
        sums[p] += fold(e, jnp.add)

    @pl.loop(0, pairs)
    def _(p):
        e = jnp.exp(own_s[p] - tops[p])
        inv = 1.0 / (spread_rows(sums[p], jnp.sum) + e)
        sums[p] = inv
        own_w[p] = e * inv

    def back_copy(which, j, peer, src, dst):
        return pltpu.make_async_remote_copy(
            src_ref=src.at[j], dst_ref=dst.at[j],
            send_sem=rsend.at[which, j], recv_sem=rrecv.at[which, j],
            device_id={"dom": peer}, device_id_type=MESH,
        )

    def term(dst, j, p, left_t, x):
        for h in range(2):
            at = pl.ds(pl.multiple_of(p * LANES + h * half, half), half)
            y = dot(left_t[at, :], x[:, h * rows:(h + 1) * rows], NN)
            dst[j, at, :] = y.astype(BF16)

    def edge_rows(base, p, x):
        x = x.astype(F32)
        for h in range(2):
            y = jnp.sum(x[:, h * rows:(h + 1) * rows], axis=0, keepdims=True)
            edge_acc[pl.ds(base + 2 * p + h, 1), :] = y

    edge_acc[...] = jnp.zeros_like(edge_acc)

    def value_block(j):
        @pl.loop(0, pairs)
        def _(p):
            wb = (score[j, p] * wide(sums[p])).astype(BF16)
            weight[j, p] = wb
            term(v_terms, j, p, g_t, wb)

    v_copies = []
    for j in (3, 1, 2):
        value_block(j)
        v_copies.append(back_copy(0, j, peers[j], v_terms, v_back))
        v_copies[-1].start()
        if j == 3:
            swaps[1][1](0)
            for t in (2, 3):
                swaps[t][0]()
    value_block(0)

    @pl.loop(0, pairs)
    def _(p):
        wb = (score[edge_block, p] * wide(sums[p])).astype(BF16)
        weight[edge_block, p] = wb
        edge_rows(0, p, wb)

    for stage in range(1, bits):
        swaps[1][1](stage)
    local_v.wait()
    for move in v_moves[2:]:
        move.wait_recv()

    @pl.loop(0, (domains + 1) * pairs)
    def _(i):
        j, p = i // pairs, i % pairs
        at = lanes_of(p)
        out_acc[:, at] += dot(weight[j, p], split(values[j, :, at]), NN)

    @pl.loop(0, pairs)
    def _(p):
        at = lanes_of(p)
        own = own_w[p]
        wb = by_lane(own).astype(BF16).astype(F32)
        v, g = v_ref[:, at].astype(F32), g_ref[:, at].astype(F32)
        out = out_acc[:, at] + wb * v
        att_ref[:, at] = out.astype(BF16)
        d = head_sums(g * out)
        delta[p] = d
        own_s[p] = own * (head_sums(g * v) - d)

    def slope(j, p):
        at = lanes_of(p)
        drop = dot(g_ref[:, at], split(values[j, :, at]), NT)
        w = score[j, p] * wide(sums[p])
        ds = (w * (drop - wide(delta[p]))).astype(BF16)
        q_acc[:, at] += dot(ds, split(keys[j, :, at]), NN)
        return ds

    def key_block(j):
        @pl.loop(0, pairs)
        def _(p):
            term(k_terms, j, p, q_t, slope(j, p))

    k_copies = []
    for j in (3, 1, 2):
        key_block(j)
        k_copies.append(back_copy(1, j, peers[j], k_terms, k_back))
        k_copies[-1].start()

    @pl.loop(0, pairs)
    def _(p):
        edge_rows(HEADS, p, slope(edge_block, p))

    edge_send[...] = dot(eye[...], edge_acc[...].astype(BF16), NT).astype(BF16)
    edge_swap = exchange(4, edge_send, edge_recv, edge_held, edge_far)
    edge_swap[0]()
    key_block(0)

    @pl.loop(0, pairs)
    def _(p):
        at = lanes_of(p)
        ds = by_lane(own_s[p]).astype(BF16).astype(F32)
        wb = by_lane(own_w[p]).astype(BF16).astype(F32)
        gq_ref[:, at] = (
            scale * (q_acc[:, at] + ds * k_ref[:, at].astype(F32))
        ).astype(BF16)
        q_acc[:, at] = ds * qs[:, at].astype(F32)
        out_acc[:, at] = wb * g_ref[:, at].astype(F32)

    for stage in range(bits):
        for swap in (swaps[2], swaps[3], edge_swap):
            swap[1](stage)

    col = lax.broadcasted_iota(jnp.int32, (LANES, width), 1) // half
    head = lax.broadcasted_iota(jnp.int32, (LANES, width), 0)
    for which, acc in ((0, out_acc), (1, q_acc)):
        grow = (head == col + which * HEADS).astype(BF16)
        piece = dot(edge_far[...], grow, NN) * far[1 - which].astype(F32)
        acc[...] += dot(hot[...], piece.astype(BF16), NN)

    for copy in v_copies:
        copy.wait_recv()
    for terms, back, acc, dst in (
        (v_terms, v_back, out_acc, gv_ref), (k_terms, k_back, q_acc, gk_ref)
    ):
        if dst is gk_ref:
            for copy in k_copies:
                copy.wait_recv()

        total = terms[0].astype(F32)
        for j in range(1, domains):
            total = total + back[j].astype(F32)
        dst[...] = (acc[...] + jnp.transpose(total)).astype(BF16)

    for copy in k_moves + v_moves + v_copies + k_copies:
        copy.wait_send()
    for swap in swaps + [edge_swap]:
        swap[2]()


def hand_out(*refs):
    copies = [
        pltpu.make_async_copy(refs[i], refs[4 + i], refs[8].at[i]) for i in range(4)
    ]
    for copy in copies:
        copy.start()
    for copy in copies:
        copy.wait()


def fused(
    n_top, groups, domains, matches, scale, query, key, value, cotangent,
    tile_index, tile_mask, tile_count, partner, near,
):
    rows, width = query.shape
    edges = matches * near.shape[2]
    pairs = width // LANES
    bits = groups.bit_length() - 1
    stats = pltpu.VMEM((pairs, rows, 2 * LANES), F32)
    wide = pltpu.VMEM((rows, width), F32)
    terms = pltpu.VMEM((domains, width, rows), BF16)
    DMA = pltpu.SemaphoreType.DMA

    def call(tops):
        return pl.pallas_call(
            functools.partial(fused_kernel, tops, scale),
            out_shape=(jax.ShapeDtypeStruct((rows, width), BF16),) * 4,
            in_specs=[SM, SM, SM] + [VM] * 6,
            out_specs=(VM,) * 4,
            scratch_shapes=[
                pltpu.VMEM((domains + 1, rows, width), BF16),
                pltpu.VMEM((domains + 1, rows, width), BF16),
                pltpu.VMEM((domains + 1, pairs, rows, 2 * rows), F32),
                pltpu.VMEM((domains + 1, pairs, rows, 2 * rows), BF16),
                pltpu.VMEM((domains + 1, rows, rows), F32),
                pltpu.VMEM((rows, width), BF16),
                pltpu.VMEM((width, rows), BF16),
                pltpu.VMEM((width, rows), BF16),
                pltpu.VMEM((rows, edges), BF16),
                pltpu.VMEM((rows, edges), BF16),
                stats, stats, stats, stats, stats,
                wide, wide,
                terms, terms, terms, terms,
                pltpu.VMEM((4, edges, width), BF16),
                pltpu.VMEM((2, edges, width), BF16),
                pltpu.VMEM((4, bits, edges, width), BF16),
                pltpu.VMEM((4, bits - 1, edges, width), BF16),
                pltpu.VMEM((matches, width), jnp.int32),
                pltpu.VMEM((LANES, edges), F32),
                pltpu.VMEM((edges, LANES), BF16),
                pltpu.VMEM((bits, edges, LANES), BF16),
                pltpu.VMEM((bits - 1, edges, LANES), BF16),
                pltpu.VMEM((edges, LANES), BF16),
                DMA((12,)), DMA((12,)),
                DMA((2, domains)), DMA((2, domains)),
                DMA((5, bits * matches)), DMA((5, bits * matches)),
                DMA((2,)),
            ],
            compiler_params=pltpu.CompilerParams(
                collective_id=tops - 1, has_side_effects=True, vmem_limit_bytes=60 << 20
            ),
            name="fused" + str(tops),
        )

    branches = [call(tops) for tops in range(1, matches + 1)]
    results = lax.switch(
        n_top - 1, branches, tile_index, tile_count, partner, near,
        query, key, value, cotangent, tile_mask,
    )
    return pl.pallas_call(
        hand_out,
        out_shape=(jax.ShapeDtypeStruct((rows, width), BF16),) * 4,
        in_specs=[VM] * 4,
        out_specs=(ANY,) * 4,
        scratch_shapes=[DMA((4,))],
        name="hand_out",
    )(*results)


def body(query, key, value, cotangent, tile_index, tile_mask, tile_count, partner, pair_edges):
    node_rows, width = query.shape
    head_size = width // HEADS
    scale = 1.0 / math.sqrt(head_size)
    domains = lax.axis_size("dom")
    groups = lax.axis_size("grp")
    matches, expander = pair_edges.shape[1], pair_edges.shape[2]
    edges = matches * expander
    tile = tile_mask.shape[2]
    slots = tile_mask.shape[1]
    blocks = node_rows // tile
    edge_blocks = edges // tile
    pairs = width // LANES
    codes = jnp.bitwise_xor(partner[0] // domains, lax.axis_index("grp"))
    n_top = jnp.sum((codes >= groups // 2).astype(jnp.int32))
    near_ids = jnp.transpose(pair_edges[0], (0, 2, 1))
    if domains == 4 and groups > 4 and blocks == 2 and edges == node_rows:
        return fused(
            n_top, groups, domains, matches, scale, query, key, value, cotangent,
            jnp.transpose(tile_index, (2, 0, 1)), tile_mask[0], tile_count, partner, near_ids,
        )
    pair_rows = jax.ShapeDtypeStruct((2, edges, width), BF16)
    send, near, code = pl.pallas_call(
        functools.partial(pick_kernel, groups, domains),
        out_shape=(
            pair_rows,
            jax.ShapeDtypeStruct((matches, expander), jnp.int32),
            jax.ShapeDtypeStruct((matches, width), jnp.int32),
        ),
        in_specs=[SM, VM, VM, VM],
        out_specs=(VM, VM, VM),
        name="pick_rows",
    )(partner, near_ids, key, value)
    group_key, group_value, far = comm(
        True, 0, groups, domains, matches, n_top, key, value, send, code
    )
    own_shape = jax.ShapeDtypeStruct((node_rows, width), BF16)
    group_blocks = domains * blocks
    tiles = slots + blocks + blocks * edge_blocks
    sources = (group_blocks + blocks + edge_blocks) * tile
    attended, grad_query, key_term, value_term, back, own_terms = pl.pallas_call(
        functools.partial(attend_kernel, scale),
        out_shape=(
            own_shape,
            own_shape,
            jax.ShapeDtypeStruct((domains * node_rows, width), BF16),
            jax.ShapeDtypeStruct((domains * node_rows, width), BF16),
            pair_rows,
            jax.ShapeDtypeStruct((2, node_rows, width), F32),
        ),
        in_specs=[SM, SM] + [VM] * 7,
        out_specs=(VM,) * 6,
        scratch_shapes=[
            pltpu.SMEM((tiles, 3), jnp.int32),
            pltpu.VMEM((tiles, tile, tile), jnp.int32),
            pltpu.VMEM((tiles, pairs, tile, 2 * tile), F32),
            pltpu.VMEM((blocks, pairs, tile, 2 * tile), F32),
            pltpu.VMEM((blocks, pairs, tile, 2 * tile), F32),
            pltpu.VMEM((node_rows, width), F32),
            pltpu.VMEM((node_rows, width), F32),
            pltpu.VMEM((sources, width), F32),
            pltpu.VMEM((sources, width), F32),
        ],
        compiler_params=pltpu.CompilerParams(vmem_limit_bytes=60 << 20),
        name="attend",
    )(
        jnp.transpose(tile_index, (2, 0, 1)), tile_count, near, query, cotangent,
        group_key, group_value, far, tile_mask[0],
    )
    key_parts, value_parts, returned = comm(
        False, matches, groups, domains, matches, n_top, key_term, value_term, back, code
    )
    grad_key, grad_value = pl.pallas_call(
        functools.partial(finish_kernel, domains),
        out_shape=(own_shape, own_shape),
        in_specs=[VM] * 5,
        out_specs=(VM, VM),
        name="finish",
    )(near, key_parts, value_parts, returned, own_terms)
    return attended, grad_query, grad_key, grad_value


def solution(mesh):
    nodes = P(("grp", "dom"), None)
    return jax.shard_map(
        body,
        mesh=mesh,
        in_specs=(
            nodes, nodes, nodes, nodes,
            P(("grp", "dom"), None, None),
            P(("grp", "dom"), None, None, None),
            P(("grp", "dom")),
            nodes,
            P(("grp", "dom"), None, None, None),
        ),
        out_specs=(nodes, nodes, nodes, nodes),
        check_vma=False,
    )
```

```python
import functools
import math
from types import SimpleNamespace as Namespace

import jax
import jax.numpy as jnp
from jax import lax
from jax.experimental import pallas as pl
from jax.experimental.pallas import tpu as pltpu
from jax.sharding import PartitionSpec as P

HEADS = 8
LANES = 128
VM = pl.BlockSpec(memory_space=pltpu.VMEM)
SM = pl.BlockSpec(memory_space=pltpu.SMEM)
ANY = pl.BlockSpec(memory_space=pl.ANY)
MESH = pl.DeviceIdType.MESH
F32 = jnp.float32
BF16 = jnp.bfloat16


def dot(a, b, dims):
    return lax.dot_general(a, b, (dims, ((), ())), preferred_element_type=F32)


NN = ((1,), (0,))
NT = ((1,), (1,))
TN = ((0,), (0,))


def pick_kernel(
    groups, domains, partner_ref, near_ref, key_ref, value_ref, out_ref, near_out, code_out
):
    matches, _, span = near_ref.shape
    rows = key_ref.shape[0]
    grp = lax.axis_index("grp")
    codes = [jnp.bitwise_xor(partner_ref[0, m] // domains, grp) for m in range(matches)]
    kinds = [
        jnp.where(c == groups // 2, 0, jnp.where(c > groups // 2, 1, 2)) for c in codes
    ]
    row_id = lax.broadcasted_iota(jnp.int32, (rows, span), 0)
    for m in range(matches):
        rank = jnp.int32(0)
        for o in range(matches):
            ahead = kinds[o] <= kinds[m] if o < m else kinds[o] < kinds[m]
            if o != m:
                rank = rank + ahead.astype(jnp.int32)
        near = near_ref[m, 0:1, :]
        near_out[pl.ds(rank, 1), :] = near
        code_out[pl.ds(rank, 1), :] = jnp.full((1, code_out.shape[1]), codes[m], jnp.int32)
        hot = (near == row_id).astype(BF16)
        at = pl.ds(pl.multiple_of(rank * span, span), span)
        out_ref[0, at, :] = dot(hot, key_ref[...], TN).astype(BF16)
        out_ref[1, at, :] = dot(hot, value_ref[...], TN).astype(BF16)


def flipped(me, bit):
    step = 1 << bit
    return me + step * (1 - 2 * ((me // step) % 2))


def comm_kernel(
    spread, n_top, groups, domains, matches, a_ref, b_ref, send_ref, code_ref,
    outa_ref, outb_ref, far_ref, recv, held, dsend, drecv, esend, erecv, lsem,
):
    dom = lax.axis_index("dom")
    grp = lax.axis_index("grp")
    rows = outa_ref.shape[0] // domains
    bits = groups.bit_length() - 1
    span = send_ref.shape[1] // matches
    barrier = pltpu.get_barrier_semaphore()
    for d in range(1, domains):
        pl.semaphore_signal(
            barrier, inc=1, device_id={"dom": lax.rem(dom + d, domains)}, device_id_type=MESH
        )
    for bit in range(bits):
        pl.semaphore_signal(
            barrier, inc=1, device_id={"grp": flipped(grp, bit)}, device_id_type=MESH
        )
    pl.semaphore_wait(barrier, domains - 1 + bits)

    def swap(stage, slot, src, dst):
        at = stage * matches + slot
        return pltpu.make_async_remote_copy(
            src_ref=src,
            dst_ref=dst,
            send_sem=esend.at[at],
            recv_sem=erecv.at[at],
            device_id={"grp": flipped(grp, bits - 1 - stage)},
            device_id_type=MESH,
        )

    def part(ref, slot):
        return ref.at[:, pl.ds(slot * span, span), :]

    moves = {}
    for slot in list(range(1, matches)) + [0]:
        first = 0 if slot < n_top else 1
        dst = part(far_ref, 0) if slot == 0 else part(recv.at[first], slot)
        moves[first, slot] = swap(first, slot, part(send_ref, slot), dst)
        moves[first, slot].start()
    mine = pl.ds(pl.multiple_of(dom * rows, rows), rows)
    locals_ = []
    spreads = []
    relay = spread and domains == 4
    near_x, near_y = flipped(dom, 0), flipped(dom, 1)

    def send_block(at, src, dst, owner, peer):
        there = pl.ds(pl.multiple_of(owner * rows, rows), rows)
        copy = pltpu.make_async_remote_copy(
            src_ref=src,
            dst_ref=dst.at[there, :],
            send_sem=dsend.at[at],
            recv_sem=drecv.at[at],
            device_id={"dom": peer},
            device_id_type=MESH,
        )
        copy.start()
        return copy

    if relay:
        a_x = send_block(0, a_ref, outa_ref, dom, near_x)
        b_y = send_block(1, b_ref, outb_ref, dom, near_y)
        b_x = send_block(2, b_ref, outb_ref, dom, near_x)
        a_y = send_block(3, a_ref, outa_ref, dom, near_y)
        spreads += [b_x, a_y]
    for which, (src, dst) in enumerate(((a_ref, outa_ref), (b_ref, outb_ref))):
        own = src if spread else src.at[mine, :]
        locals_.append(pltpu.make_async_copy(own, dst.at[mine, :], lsem.at[which]))
        locals_[-1].start()
        for d in range(1, domains) if not relay else ():
            peer = lax.rem(dom + d, domains)
            theirs = pl.ds(pl.multiple_of(peer * rows, rows), rows)
            copy = pltpu.make_async_remote_copy(
                src_ref=src if spread else src.at[theirs, :],
                dst_ref=dst.at[mine, :],
                send_sem=dsend.at[which * domains + d],
                recv_sem=drecv.at[which * domains + d],
                device_id={"dom": peer},
                device_id_type=MESH,
            )
            copy.start()
            spreads.append(copy)
    if relay:
        from_x = pl.ds(pl.multiple_of(near_x * rows, rows), rows)
        from_y = pl.ds(pl.multiple_of(near_y * rows, rows), rows)
        a_x.wait()
        spreads.append(send_block(4, outa_ref.at[from_x, :], outa_ref, near_x, near_y))
        b_y.wait()
        spreads.append(send_block(5, outb_ref.at[from_y, :], outb_ref, near_y, near_x))
    for stage in range(bits):
        last = stage == bits - 1
        others = list(range(n_top, matches)) if stage else []
        chosen = others + list(range(1, n_top))
        for slot in chosen:
            moves[stage, slot].wait_recv()
            piece = pl.ds(slot * span, span)
            fresh = stage == (0 if slot < n_top else 1)
            source = send_ref if fresh else held.at[stage - 1]
            taken = (code_ref[slot:slot + 1, :] // (1 << (bits - 1 - stage))) % 2 == 1
            target = far_ref if last else held.at[stage]
            for half in range(2):
                target[half, piece, :] = jnp.where(
                    taken, recv[stage, half, piece, :], source[half, piece, :]
                )
            if not last:
                moves[stage + 1, slot] = swap(
                    stage + 1, slot, part(held.at[stage], slot), part(recv.at[stage + 1], slot)
                )
                moves[stage + 1, slot].start()
    moves[0, 0].wait_recv()
    for move in moves.values():
        move.wait_send()
    for copy in spreads:
        copy.wait()
    for copy in locals_:
        copy.wait()


def comm(spread, cid, groups, domains, matches, n_top, a, b, send, code):
    rows = a.shape[0] if spread else a.shape[0] // domains
    width = a.shape[1]
    bits = groups.bit_length() - 1
    whole = jax.ShapeDtypeStruct((domains * rows, width), BF16)

    def call(tops):
        return pl.pallas_call(
            functools.partial(comm_kernel, spread, tops, groups, domains, matches),
            out_shape=(whole, whole, jax.ShapeDtypeStruct(send.shape, BF16)),
            in_specs=[VM, VM, VM, VM],
            out_specs=(ANY, ANY, VM),
            scratch_shapes=[
                pltpu.VMEM((bits,) + send.shape, BF16),
                pltpu.VMEM((max(bits - 1, 1),) + send.shape, BF16),
                pltpu.SemaphoreType.DMA((2 * domains,)),
                pltpu.SemaphoreType.DMA((2 * domains,)),
                pltpu.SemaphoreType.DMA((bits * matches,)),
                pltpu.SemaphoreType.DMA((bits * matches,)),
                pltpu.SemaphoreType.DMA((2,)),
            ],
            name=("gather_rows" if spread else "return_terms") + str(tops),
            compiler_params=pltpu.CompilerParams(
                collective_id=cid + tops - 1, has_side_effects=True
            ),
        )

    branches = [call(tops) for tops in range(1, matches + 1)]
    return lax.switch(n_top - 1, branches, a, b, send, code)


def attend_kernel(
    scale, entry_ref, count_ref, near_ref, q_ref, g_ref, gk_ref, gv_ref, far_ref, mask_ref,
    att_ref, gq_ref, kt_ref, vt_ref, back_ref, self_ref,
    table, masks, store, tops, sums, out_acc, q_acc, k_acc, v_acc,
):
    tile = mask_ref.shape[1]
    node_rows, width = q_ref.shape
    blocks = node_rows // tile
    edge_blocks = far_ref.shape[1] // tile
    group_blocks = gk_ref.shape[0] // tile
    slots = mask_ref.shape[0]
    pairs = width // LANES
    fixed = blocks + blocks * edge_blocks
    dom = lax.axis_index("dom")
    low = lax.broadcasted_iota(jnp.int32, (tile, LANES), 1) < (width // HEADS)
    row_id = lax.broadcasted_iota(jnp.int32, (tile, tile), 0)
    col_id = lax.broadcasted_iota(jnp.int32, (tile, tile), 1)
    zero = jnp.zeros((tile, LANES), BF16)

    def fill(t, a, kb, gb):
        table[t, 0] = a
        table[t, 1] = kb
        table[t, 2] = gb

    k_far = group_blocks + blocks
    for a in range(blocks):
        fill(a, a, dom * blocks + a, group_blocks + a)
        masks[a] = (row_id == col_id).astype(jnp.int32)
        for e in range(edge_blocks):
            t = blocks + a * edge_blocks + e
            fill(t, a, group_blocks + e, k_far + e)
            first = e * tile // near_ref.shape[1]
            last = (e + 1) * tile // near_ref.shape[1]
            near = jnp.concatenate([near_ref[r:r + 1, :] for r in range(first, last)], axis=1)
            masks[t] = (near == row_id + a * tile).astype(jnp.int32)
    for s in range(slots):
        live = s < count_ref[0]
        kb = jnp.where(live, entry_ref[1, 0, s] * blocks + entry_ref[2, 0, s], 0)
        fill(fixed + s, jnp.where(live, entry_ref[0, 0, s], 0), kb, kb)
        masks[fixed + s] = jnp.where(live, mask_ref[s], 0)
    assert (fixed + slots) % 2 == 0
    turns = (fixed + count_ref[0] + 1) // 2

    def each_tile(work):
        @pl.loop(0, turns)
        def _(i):
            for t in (2 * i, 2 * i + 1):
                work(t)

    @pl.loop(0, k_far + edge_blocks)
    def _(i):
        at = pl.ds(pl.multiple_of(i * tile, tile), tile)
        k_acc[at, :] = jnp.zeros((tile, width), F32)
        v_acc[at, :] = jnp.zeros((tile, width), F32)

    out_acc[...] = jnp.zeros_like(out_acc)
    q_acc[...] = jnp.zeros_like(q_acc)
    tops[...] = jnp.full_like(tops, -jnp.inf)
    sums[...] = jnp.zeros_like(sums)

    def cols(p):
        return slice(p * LANES, (p + 1) * LANES)

    def rows(i):
        return pl.ds(pl.multiple_of(i * tile, tile), tile)

    def split(x):
        return jnp.concatenate([jnp.where(low, x, zero), jnp.where(low, zero, x)], axis=0)

    def stack(y):
        return jnp.concatenate([y[:, :tile], y[:, tile:]], axis=0)

    def far_or_group(which, kb, p):
        ref = (gk_ref, gv_ref)[which]
        far_at = jnp.clip(kb - group_blocks, 0, edge_blocks - 1)
        near_at = jnp.minimum(kb, group_blocks - 1)
        return jnp.where(
            kb < group_blocks,
            ref[rows(near_at), cols(p)],
            far_ref[which, rows(far_at), cols(p)],
        )

    @each_tile
    def _(t):
        a = table[t, 0]
        kb = table[t, 1]
        live = masks[t] != 0
        live2 = jnp.concatenate([live, live], axis=1)
        for p in range(pairs):
            k2 = split(far_or_group(0, kb, p))
            s2 = dot(q_ref[rows(a), cols(p)], k2, NT) * scale
            s2 = jnp.where(live2, s2, -jnp.inf)
            store[t, p] = s2
            tops[a, p] = jnp.maximum(tops[a, p], s2)

    def spread_rows(x, reduce):
        left = jnp.broadcast_to(reduce(x[:, :tile], axis=1, keepdims=True), (tile, tile))
        right = jnp.broadcast_to(reduce(x[:, tile:], axis=1, keepdims=True), (tile, tile))
        return jnp.concatenate([left, right], axis=1)

    for i in range(blocks * pairs):
        a, p = i // pairs, i % pairs
        tops[a, p] = spread_rows(tops[a, p], jnp.max)

    @each_tile
    def _(t):
        a = table[t, 0]
        for p in range(pairs):
            e2 = jnp.exp(store[t, p] - tops[a, p])
            store[t, p] = e2
            sums[a, p] += e2

    for i in range(blocks * pairs):
        a, p = i // pairs, i % pairs
        sums[a, p] = 1.0 / spread_rows(sums[a, p], jnp.sum)

    @each_tile
    def _(t):
        a = table[t, 0]
        kb = table[t, 1]
        for p in range(pairs):
            w2 = store[t, p] * sums[a, p]
            store[t, p] = w2
            v2 = split(far_or_group(1, kb, p))
            out_acc[rows(a), cols(p)] += dot(w2.astype(BF16), v2, NN)

    att_ref[...] = out_acc[...].astype(BF16)
    for a in range(blocks):
        for p in range(pairs):
            at = slice(a * tile, (a + 1) * tile)
            prod = g_ref[at, cols(p)].astype(F32) * out_acc[at, cols(p)]
            left = jnp.sum(jnp.where(low, prod, 0.0), axis=1, keepdims=True)
            right = jnp.sum(jnp.where(low, 0.0, prod), axis=1, keepdims=True)
            tops[a, p] = jnp.concatenate(
                [jnp.broadcast_to(left, (tile, tile)), jnp.broadcast_to(right, (tile, tile))],
                axis=1,
            )

    @each_tile
    def _(t):
        a = table[t, 0]
        kb = table[t, 1]
        gb = table[t, 2]
        for p in range(pairs):
            w2 = store[t, p]
            k2 = split(far_or_group(0, kb, p))
            v2 = split(far_or_group(1, kb, p))
            q = q_ref[rows(a), cols(p)]
            g = g_ref[rows(a), cols(p)]
            drop = dot(g, v2, NT)
            ds = (w2 * (drop - tops[a, p])).astype(BF16)
            q_acc[rows(a), cols(p)] += dot(ds, k2, NN)
            k_acc[rows(gb), cols(p)] += dot(stack(ds), split(q), TN)
            v_acc[rows(gb), cols(p)] += dot(stack(w2.astype(BF16)), split(g), TN)

    gq_ref[...] = (scale * q_acc[...]).astype(BF16)

    @pl.loop(0, group_blocks)
    def _(i):
        kt_ref[rows(i), :] = (scale * k_acc[rows(i), :]).astype(BF16)
        vt_ref[rows(i), :] = v_acc[rows(i), :].astype(BF16)

    own = slice(group_blocks * tile, k_far * tile)
    far = slice(k_far * tile, (k_far + edge_blocks) * tile)
    self_ref[0] = scale * k_acc[own, :]
    self_ref[1] = v_acc[own, :]
    back_ref[0] = (scale * k_acc[far, :]).astype(BF16)
    back_ref[1] = v_acc[far, :].astype(BF16)


def finish_kernel(domains, near_ref, ka_ref, va_ref, back_ref, self_ref, gk_ref, gv_ref):
    rows = gk_ref.shape[0]
    matches = near_ref.shape[0]
    near = jnp.concatenate([near_ref[m:m + 1, :] for m in range(matches)], axis=1)
    hot = (near == lax.broadcasted_iota(jnp.int32, (rows, near.shape[1]), 0)).astype(BF16)
    for which, (src, dst) in enumerate(((ka_ref, gk_ref), (va_ref, gv_ref))):
        acc = self_ref[which] + dot(hot, back_ref[which], NN)
        for d in range(domains):
            acc = acc + src[d * rows:(d + 1) * rows, :].astype(F32)
        dst[...] = acc.astype(BF16)


def lanes_of(p):
    return pl.ds(pl.multiple_of(p * LANES, LANES), LANES)


def fused_kernel(
    n_top, scale, entry_ref, count_ref, partner_ref, near_ref,
    q_ref, k_ref, v_ref, g_ref, mask_ref,
    att_ref, gq_ref, gk_ref, gv_ref,
    keys, values, score, weight, bias, qs, q_t, g_t, hot, eye,
    tops, sums, delta, own_w, own_s, out_acc, q_acc,
    v_terms, k_terms, v_back, k_back,
    pick, far, recv, held, code_rows,
    edge_acc, edge_send, edge_recv, edge_held, edge_far,
    dsend, drecv, rsend, rrecv, esend, erecv, lsem,
):
    rows, width = q_ref.shape
    domains = keys.shape[0] - 1
    matches, _, span = near_ref.shape
    edges = matches * span
    tile = mask_ref.shape[1]
    slots = mask_ref.shape[0]
    blocks = rows // tile
    pairs = width // LANES
    half = width // HEADS
    groups = lax.axis_size("grp")
    bits = groups.bit_length() - 1
    dom = lax.axis_index("dom")
    grp = lax.axis_index("grp")
    near_x, near_y, across = flipped(dom, 0), flipped(dom, 1), flipped(flipped(dom, 0), 1)
    peers = (dom, near_x, near_y, across)
    edge_block = domains

    barrier = pltpu.get_barrier_semaphore()
    for d in range(1, domains):
        pl.semaphore_signal(barrier, inc=1, device_id={"dom": peers[d]}, device_id_type=MESH)
    for bit in range(bits):
        pl.semaphore_signal(
            barrier, inc=1, device_id={"grp": flipped(grp, bit)}, device_id_type=MESH
        )

    lane = lax.broadcasted_iota(jnp.int32, (rows, LANES), 1)
    low = lane < half
    row_id = lax.broadcasted_iota(jnp.int32, (rows, edges), 0)
    col_id = lax.broadcasted_iota(jnp.int32, (rows, edges), 1)
    eye[...] = (row_id == col_id).astype(BF16)

    local_k = pltpu.make_async_copy(k_ref, keys.at[0], lsem.at[0])
    local_v = pltpu.make_async_copy(v_ref, values.at[0], lsem.at[1])

    def block(b):
        return pl.ds(b * tile, tile)

    def send(at, src, dst, peer):
        copy = pltpu.make_async_remote_copy(
            src_ref=src, dst_ref=dst, send_sem=dsend.at[at], recv_sem=drecv.at[at],
            device_id={"dom": peer}, device_id_type=MESH,
        )
        copy.start()
        return copy

    def spread(base, src, dst):
        x0 = send(base, src.at[block(0), :], dst.at[1, block(0), :], near_x)
        y1 = send(base + 1, src.at[block(1), :], dst.at[2, block(1), :], near_y)
        x1 = send(base + 2, src.at[block(1), :], dst.at[1, block(1), :], near_x)
        y0 = send(base + 3, src.at[block(0), :], dst.at[2, block(0), :], near_y)
        return [x0, y1, x1, y0]

    def relay(base, moves, dst):
        moves[0].wait_recv()
        first = send(base + 4, dst.at[1, block(0), :], dst.at[3, block(0), :], near_y)
        moves[1].wait_recv()
        second = send(base + 5, dst.at[2, block(1), :], dst.at[3, block(1), :], near_x)
        return moves + [first, second]

    pl.semaphore_wait(barrier, domains - 1 + bits)
    k_moves = spread(0, k_ref, keys)
    local_k.start()
    local_v.start()

    codes = [jnp.bitwise_xor(partner_ref[0, m] // domains, grp) for m in range(matches)]
    kinds = [
        jnp.where(c == groups // 2, 0, jnp.where(c > groups // 2, 1, 2)) for c in codes
    ]
    ranks = []
    for m in range(matches):
        rank = jnp.int32(0)
        for o in range(matches):
            ahead = kinds[o] <= kinds[m] if o < m else kinds[o] < kinds[m]
            if o != m:
                rank = rank + ahead.astype(jnp.int32)
        ranks.append(rank)
    near_parts = []
    for r in range(matches):
        code = jnp.int32(0)
        ids = jnp.zeros((1, span), jnp.int32)
        for m in range(matches):
            here = (ranks[m] == r).astype(jnp.int32)
            code = code + here * codes[m]
            ids = ids + here * near_ref[m, 0:1, :]
        near_parts.append(ids)
        code_rows[r:r + 1, :] = jnp.full((1, width), code, jnp.int32)
    near = jnp.concatenate(near_parts, axis=1)
    hot_mask = near == row_id
    hot[...] = hot_mask.astype(BF16)
    bias[edge_block] = jnp.where(hot_mask, 0.0, -jnp.inf)

    def part(ref, slot):
        return ref.at[pl.ds(slot * span, span), :]

    def exchange(kind, src, recvs, helds, dst):
        def swap(stage, slot, source, target):
            at = stage * matches + slot
            return pltpu.make_async_remote_copy(
                src_ref=source, dst_ref=target,
                send_sem=esend.at[kind, at], recv_sem=erecv.at[kind, at],
                device_id={"grp": flipped(grp, bits - 1 - stage)}, device_id_type=MESH,
            )

        moves = {}

        def start():
            for slot in list(range(1, matches)) + [0]:
                first = 0 if slot < n_top else 1
                target = part(dst, 0) if slot == 0 else part(recvs.at[first], slot)
                moves[first, slot] = swap(first, slot, part(src, slot), target)
                moves[first, slot].start()

        def step(stage):
            last = stage == bits - 1
            others = list(range(n_top, matches)) if stage else []
            for slot in others + list(range(1, n_top)):
                moves[stage, slot].wait_recv()
                piece = pl.ds(slot * span, span)
                fresh = stage == (0 if slot < n_top else 1)
                source = src if fresh else helds.at[stage - 1]
                code = code_rows[slot:slot + 1, :dst.shape[1]]
                taken = (code // (1 << (bits - 1 - stage))) % 2 == 1
                target = dst if last else helds.at[stage]
                target[piece, :] = jnp.where(
                    taken, recvs[stage, piece, :], source[piece, :]
                )
                if not last:
                    moves[stage + 1, slot] = swap(
                        stage + 1, slot, part(helds.at[stage], slot),
                        part(recvs.at[stage + 1], slot),
                    )
                    moves[stage + 1, slot].start()
            if last:
                moves[0, 0].wait_recv()

        def drain():
            for move in moves.values():
                move.wait_send()

        return start, step, drain

    def exchange_low(kind, src, recvs, helds, dst):
        top = bits - 1
        moves = {}

        def swap(stage, slot, source, target):
            at = stage * matches + slot
            moves[stage, slot] = pltpu.make_async_remote_copy(
                src_ref=part(source, slot), dst_ref=part(target, slot),
                send_sem=esend.at[kind, at], recv_sem=erecv.at[kind, at],
                device_id={"grp": flipped(grp, stage)}, device_id_type=MESH,
            )
            moves[stage, slot].start()

        def start():
            for slot in range(1, matches):
                swap(0, slot, src, recvs.at[0])

        def first():
            swap(top, 0, src, dst)

        def pick_up(stage):
            for slot in range(1, matches):
                moves[stage, slot].wait_recv()
                piece = pl.ds(slot * span, span)
                source = helds.at[stage - 1] if stage else src
                code = code_rows[slot:slot + 1, :dst.shape[1]]
                taken = (code // (1 << stage)) % 2 == 1
                final = stage == top - 1 and slot >= n_top
                target = dst if final else helds.at[stage]
                target[piece, :] = jnp.where(
                    taken, recvs[stage, piece, :], source[piece, :]
                )

        def pass_on(stage):
            last = stage == top - 1
            for slot in range(1, n_top if last else matches):
                swap(stage + 1, slot, helds.at[stage], dst if last else recvs.at[stage + 1])

        def finish():
            for slot in range(n_top):
                moves[top, slot].wait_recv()

        def drain():
            for move in moves.values():
                move.wait_send()

        return Namespace(
            start=start, first=first, pick_up=pick_up, pass_on=pass_on, finish=finish, drain=drain
        )

    far_refs = (keys.at[edge_block], values.at[edge_block], far.at[0], far.at[1])
    swaps = [
        exchange(t, pick.at[t], recv.at[t], held.at[t], far_refs[t]) for t in range(2)
    ]
    q_swap, g_swap = [
        exchange_low(t, pick.at[t], recv.at[t], held.at[t], far_refs[t]) for t in (2, 3)
    ]
    edge_swap = exchange_low(4, edge_send, edge_recv, edge_held, edge_far)
    lower = range(1, bits - 1)

    hot_t = dot(eye[...], hot[...], NT).astype(BF16)
    for t, src in enumerate((k_ref, v_ref)):
        pick[t] = dot(hot_t, src[...], NN).astype(BF16)
        swaps[t][0]()

    qs[...] = (q_ref[...].astype(F32) * scale).astype(BF16)
    pick[2] = dot(hot_t, qs[...], NN).astype(BF16)
    pick[3] = dot(hot_t, g_ref[...], NN).astype(BF16)
    q_swap.start()
    g_swap.start()
    k_moves = relay(0, k_moves, keys)
    v_moves = spread(6, v_ref, values)
    q_t[...] = jnp.transpose(qs[...].astype(F32)).astype(BF16)
    g_t[...] = jnp.transpose(g_ref[...].astype(F32)).astype(BF16)

    @pl.loop(0, domains * blocks * blocks)
    def _(i):
        j, a, b = i // (blocks * blocks), (i // blocks) % blocks, i % blocks
        c = (dom + j) % 2 + 2 * ((dom // 2 + j // 2) % 2)
        at, live = jnp.int32(0), jnp.int32(0)
        for s in range(slots):
            hit = (entry_ref[0, 0, s] == a) & (entry_ref[1, 0, s] == c)
            hit = (hit & (entry_ref[2, 0, s] == b) & (s < count_ref[0])).astype(jnp.int32)
            at = at + hit * s
            live = live + hit
        seen = mask_ref[at] * live
        ra = pl.ds(pl.multiple_of(a * tile, tile), tile)
        rb = pl.ds(pl.multiple_of(b * tile, tile), tile)
        bias[j, ra, rb] = jnp.where(seen != 0, 0.0, -jnp.inf)

    zero = jnp.zeros((rows, LANES), BF16)

    def split(x):
        return jnp.concatenate([jnp.where(low, x, zero), jnp.where(low, zero, x)], axis=0)

    def wide(x):
        left, right = x[:, :LANES], x[:, LANES:]
        return jnp.concatenate([left, left, right, right], axis=1)

    def fold(x, op):
        n = rows // LANES
        out = []
        for h in range(2):
            at = h * rows
            y = x[:, at:at + LANES]
            for i in range(1, n):
                y = op(y, x[:, at + i * LANES:at + (i + 1) * LANES])
            out.append(y)
        return jnp.concatenate(out, axis=1)

    def spread_rows(x, reduce):
        left = jnp.broadcast_to(reduce(x[:, :LANES], axis=1, keepdims=True), (rows, LANES))
        right = jnp.broadcast_to(reduce(x[:, LANES:], axis=1, keepdims=True), (rows, LANES))
        return jnp.concatenate([left, right], axis=1)

    def head_sums(x):
        left = jnp.sum(jnp.where(low, x, 0.0), axis=1, keepdims=True)
        right = jnp.sum(jnp.where(low, 0.0, x), axis=1, keepdims=True)
        return jnp.concatenate(
            [jnp.broadcast_to(left, (rows, LANES)), jnp.broadcast_to(right, (rows, LANES))],
            axis=1,
        )

    def by_lane(x):
        return jnp.where(low, x[:, :LANES], x[:, LANES:])

    def score_block(j):
        @pl.loop(0, pairs)
        def _(p):
            at = lanes_of(p)
            s = dot(qs[:, at], split(keys[j, :, at]), NT)
            b = bias[j]
            s = s + jnp.concatenate([b, b], axis=1)
            score[j, p] = s
            tops[p] = jnp.maximum(tops[p], fold(s, jnp.maximum))

    @pl.loop(0, pairs)
    def _(p):
        at = lanes_of(p)
        own = head_sums(qs[:, at].astype(F32) * k_ref[:, at].astype(F32))
        own_s[p] = own
        tops[p] = own
        sums[p] = jnp.zeros((rows, 2 * LANES), F32)
        out_acc[:, at] = jnp.zeros((rows, LANES), F32)
        q_acc[:, at] = jnp.zeros((rows, LANES), F32)

    local_k.wait()
    score_block(0)
    k_moves[2].wait_recv()
    score_block(1)
    k_moves[3].wait_recv()
    score_block(2)
    swaps[0][1](0)
    k_moves[4].wait_recv()
    k_moves[5].wait_recv()
    score_block(3)
    q_swap.pick_up(0)
    g_swap.pick_up(0)
    v_moves = relay(6, v_moves, values)
    for stage in range(1, bits):
        swaps[0][1](stage)
    score_block(edge_block)

    @pl.loop(0, pairs)
    def _(p):
        tops[p] = spread_rows(tops[p], jnp.max)

    @pl.loop(0, (domains + 1) * pairs)
    def _(i):
        j, p = i // pairs, i % pairs
        e = jnp.exp(score[j, p] - wide(tops[p]))
        score[j, p] = e
        sums[p] += fold(e, jnp.add)

    @pl.loop(0, pairs)
    def _(p):
        e = jnp.exp(own_s[p] - tops[p])
        inv = 1.0 / (spread_rows(sums[p], jnp.sum) + e)
        sums[p] = inv
        own_w[p] = e * inv

    def back_copy(which, j, peer, src, dst):
        return pltpu.make_async_remote_copy(
            src_ref=src.at[j], dst_ref=dst.at[j],
            send_sem=rsend.at[which, j], recv_sem=rrecv.at[which, j],
            device_id={"dom": peer}, device_id_type=MESH,
        )

    def term(dst, j, p, left_t, x):
        for h in range(2):
            at = pl.ds(pl.multiple_of(p * LANES + h * half, half), half)
            y = dot(left_t[at, :], x[:, h * rows:(h + 1) * rows], NN)
            dst[j, at, :] = y.astype(BF16)

    def edge_rows(base, p, x):
        x = x.astype(F32)
        for h in range(2):
            y = jnp.sum(x[:, h * rows:(h + 1) * rows], axis=0, keepdims=True)
            edge_acc[pl.ds(base + 2 * p + h, 1), :] = y

    edge_acc[...] = jnp.zeros_like(edge_acc)

    def value_block(j):
        @pl.loop(0, pairs)
        def _(p):
            wb = (score[j, p] * wide(sums[p])).astype(BF16)
            weight[j, p] = wb
            term(v_terms, j, p, g_t, wb)

    v_copies = []
    for j in (3, 1, 2):
        value_block(j)
        v_copies.append(back_copy(0, j, peers[j], v_terms, v_back))
        v_copies[-1].start()
        if j == 3:
            swaps[1][1](0)
            q_swap.pass_on(0)
            g_swap.pass_on(0)
            q_swap.first()
            g_swap.first()
    value_block(0)

    @pl.loop(0, pairs)
    def _(p):
        wb = (score[edge_block, p] * wide(sums[p])).astype(BF16)
        weight[edge_block, p] = wb
        edge_rows(0, p, wb)

    for stage in range(1, bits):
        swaps[1][1](stage)
    local_v.wait()
    for move in v_moves[2:]:
        move.wait_recv()

    @pl.loop(0, (domains + 1) * pairs)
    def _(i):
        j, p = i // pairs, i % pairs
        at = lanes_of(p)
        out_acc[:, at] += dot(weight[j, p], split(values[j, :, at]), NN)

    @pl.loop(0, pairs)
    def _(p):
        at = lanes_of(p)
        own = own_w[p]
        wb = by_lane(own).astype(BF16).astype(F32)
        v, g = v_ref[:, at].astype(F32), g_ref[:, at].astype(F32)
        out = out_acc[:, at] + wb * v
        att_ref[:, at] = out.astype(BF16)
        d = head_sums(g * out)
        delta[p] = d
        own_s[p] = own * (head_sums(g * v) - d)

    def slope(j, p):
        at = lanes_of(p)
        drop = dot(g_ref[:, at], split(values[j, :, at]), NT)
        w = score[j, p] * wide(sums[p])
        ds = (w * (drop - wide(delta[p]))).astype(BF16)
        q_acc[:, at] += dot(ds, split(keys[j, :, at]), NN)
        return ds

    def key_block(j):
        @pl.loop(0, pairs)
        def _(p):
            term(k_terms, j, p, q_t, slope(j, p))

    k_copies = []
    for j in (3, 1, 2):
        key_block(j)
        k_copies.append(back_copy(1, j, peers[j], k_terms, k_back))
        k_copies[-1].start()
        if j == 3:
            @pl.loop(0, pairs)
            def _(p):
                edge_rows(HEADS, p, slope(edge_block, p))

            edge_send[...] = dot(eye[...], edge_acc[...].astype(BF16), NT).astype(BF16)
            edge_swap.start()
        if j == 1:
            edge_swap.pick_up(0)
            edge_swap.pass_on(0)
        if j == 3:
            for swap in (q_swap, g_swap):
                for stage in lower:
                    swap.pick_up(stage)
                    swap.pass_on(stage)
    key_block(0)
    for stage in lower:
        edge_swap.pick_up(stage)
        edge_swap.pass_on(stage)
    edge_swap.first()

    @pl.loop(0, pairs)
    def _(p):
        at = lanes_of(p)
        ds = by_lane(own_s[p]).astype(BF16).astype(F32)
        wb = by_lane(own_w[p]).astype(BF16).astype(F32)
        gq_ref[:, at] = (
            scale * (q_acc[:, at] + ds * k_ref[:, at].astype(F32))
        ).astype(BF16)
        q_acc[:, at] = ds * qs[:, at].astype(F32)
        out_acc[:, at] = wb * g_ref[:, at].astype(F32)

    for swap in (q_swap, g_swap, edge_swap):
        swap.finish()

    col = lax.broadcasted_iota(jnp.int32, (LANES, width), 1) // half
    head = lax.broadcasted_iota(jnp.int32, (LANES, width), 0)
    for which, acc in ((0, out_acc), (1, q_acc)):
        grow = (head == col + which * HEADS).astype(BF16)
        piece = dot(edge_far[...], grow, NN) * far[1 - which].astype(F32)
        acc[...] += dot(hot[...], piece.astype(BF16), NN)

    for copy in v_copies:
        copy.wait_recv()
    for terms, back, acc, dst in (
        (v_terms, v_back, out_acc, gv_ref), (k_terms, k_back, q_acc, gk_ref)
    ):
        if dst is gk_ref:
            for copy in k_copies:
                copy.wait_recv()

        total = terms[0].astype(F32)
        for j in range(1, domains):
            total = total + back[j].astype(F32)
        dst[...] = (acc[...] + jnp.transpose(total)).astype(BF16)

    for copy in k_moves + v_moves + v_copies + k_copies:
        copy.wait_send()
    for swap in swaps:
        swap[2]()
    for swap in (q_swap, g_swap, edge_swap):
        swap.drain()


def hand_out(*refs):
    copies = [
        pltpu.make_async_copy(refs[i], refs[4 + i], refs[8].at[i]) for i in range(4)
    ]
    for copy in copies:
        copy.start()
    for copy in copies:
        copy.wait()


def fused(
    n_top, groups, domains, matches, scale, query, key, value, cotangent,
    tile_index, tile_mask, tile_count, partner, near,
):
    rows, width = query.shape
    edges = matches * near.shape[2]
    pairs = width // LANES
    bits = groups.bit_length() - 1
    stats = pltpu.VMEM((pairs, rows, 2 * LANES), F32)
    wide = pltpu.VMEM((rows, width), F32)
    terms = pltpu.VMEM((domains, width, rows), BF16)
    DMA = pltpu.SemaphoreType.DMA

    def call(tops):
        return pl.pallas_call(
            functools.partial(fused_kernel, tops, scale),
            out_shape=(jax.ShapeDtypeStruct((rows, width), BF16),) * 4,
            in_specs=[SM, SM, SM] + [VM] * 6,
            out_specs=(VM,) * 4,
            scratch_shapes=[
                pltpu.VMEM((domains + 1, rows, width), BF16),
                pltpu.VMEM((domains + 1, rows, width), BF16),
                pltpu.VMEM((domains + 1, pairs, rows, 2 * rows), F32),
                pltpu.VMEM((domains + 1, pairs, rows, 2 * rows), BF16),
                pltpu.VMEM((domains + 1, rows, rows), F32),
                pltpu.VMEM((rows, width), BF16),
                pltpu.VMEM((width, rows), BF16),
                pltpu.VMEM((width, rows), BF16),
                pltpu.VMEM((rows, edges), BF16),
                pltpu.VMEM((rows, edges), BF16),
                stats, stats, stats, stats, stats,
                wide, wide,
                terms, terms, terms, terms,
                pltpu.VMEM((4, edges, width), BF16),
                pltpu.VMEM((2, edges, width), BF16),
                pltpu.VMEM((4, bits, edges, width), BF16),
                pltpu.VMEM((4, bits - 1, edges, width), BF16),
                pltpu.VMEM((matches, width), jnp.int32),
                pltpu.VMEM((LANES, edges), F32),
                pltpu.VMEM((edges, LANES), BF16),
                pltpu.VMEM((bits, edges, LANES), BF16),
                pltpu.VMEM((bits - 1, edges, LANES), BF16),
                pltpu.VMEM((edges, LANES), BF16),
                DMA((12,)), DMA((12,)),
                DMA((2, domains)), DMA((2, domains)),
                DMA((5, bits * matches)), DMA((5, bits * matches)),
                DMA((2,)),
            ],
            compiler_params=pltpu.CompilerParams(
                collective_id=tops - 1, has_side_effects=True, vmem_limit_bytes=60 << 20
            ),
            name="fused" + str(tops),
        )

    branches = [call(tops) for tops in range(1, matches + 1)]
    results = lax.switch(
        n_top - 1, branches, tile_index, tile_count, partner, near,
        query, key, value, cotangent, tile_mask,
    )
    return pl.pallas_call(
        hand_out,
        out_shape=(jax.ShapeDtypeStruct((rows, width), BF16),) * 4,
        in_specs=[VM] * 4,
        out_specs=(ANY,) * 4,
        scratch_shapes=[DMA((4,))],
        name="hand_out",
    )(*results)


def body(query, key, value, cotangent, tile_index, tile_mask, tile_count, partner, pair_edges):
    node_rows, width = query.shape
    head_size = width // HEADS
    scale = 1.0 / math.sqrt(head_size)
    domains = lax.axis_size("dom")
    groups = lax.axis_size("grp")
    matches, expander = pair_edges.shape[1], pair_edges.shape[2]
    edges = matches * expander
    tile = tile_mask.shape[2]
    slots = tile_mask.shape[1]
    blocks = node_rows // tile
    edge_blocks = edges // tile
    pairs = width // LANES
    codes = jnp.bitwise_xor(partner[0] // domains, lax.axis_index("grp"))
    n_top = jnp.sum((codes >= groups // 2).astype(jnp.int32))
    near_ids = jnp.transpose(pair_edges[0], (0, 2, 1))
    if domains == 4 and groups > 4 and blocks == 2 and edges == node_rows:
        return fused(
            n_top, groups, domains, matches, scale, query, key, value, cotangent,
            jnp.transpose(tile_index, (2, 0, 1)), tile_mask[0], tile_count, partner, near_ids,
        )
    pair_rows = jax.ShapeDtypeStruct((2, edges, width), BF16)
    send, near, code = pl.pallas_call(
        functools.partial(pick_kernel, groups, domains),
        out_shape=(
            pair_rows,
            jax.ShapeDtypeStruct((matches, expander), jnp.int32),
            jax.ShapeDtypeStruct((matches, width), jnp.int32),
        ),
        in_specs=[SM, VM, VM, VM],
        out_specs=(VM, VM, VM),
        name="pick_rows",
    )(partner, near_ids, key, value)
    group_key, group_value, far = comm(
        True, 0, groups, domains, matches, n_top, key, value, send, code
    )
    own_shape = jax.ShapeDtypeStruct((node_rows, width), BF16)
    group_blocks = domains * blocks
    tiles = slots + blocks + blocks * edge_blocks
    sources = (group_blocks + blocks + edge_blocks) * tile
    attended, grad_query, key_term, value_term, back, own_terms = pl.pallas_call(
        functools.partial(attend_kernel, scale),
        out_shape=(
            own_shape,
            own_shape,
            jax.ShapeDtypeStruct((domains * node_rows, width), BF16),
            jax.ShapeDtypeStruct((domains * node_rows, width), BF16),
            pair_rows,
            jax.ShapeDtypeStruct((2, node_rows, width), F32),
        ),
        in_specs=[SM, SM] + [VM] * 7,
        out_specs=(VM,) * 6,
        scratch_shapes=[
            pltpu.SMEM((tiles, 3), jnp.int32),
            pltpu.VMEM((tiles, tile, tile), jnp.int32),
            pltpu.VMEM((tiles, pairs, tile, 2 * tile), F32),
            pltpu.VMEM((blocks, pairs, tile, 2 * tile), F32),
            pltpu.VMEM((blocks, pairs, tile, 2 * tile), F32),
            pltpu.VMEM((node_rows, width), F32),
            pltpu.VMEM((node_rows, width), F32),
            pltpu.VMEM((sources, width), F32),
            pltpu.VMEM((sources, width), F32),
        ],
        compiler_params=pltpu.CompilerParams(vmem_limit_bytes=60 << 20),
        name="attend",
    )(
        jnp.transpose(tile_index, (2, 0, 1)), tile_count, near, query, cotangent,
        group_key, group_value, far, tile_mask[0],
    )
    key_parts, value_parts, returned = comm(
        False, matches, groups, domains, matches, n_top, key_term, value_term, back, code
    )
    grad_key, grad_value = pl.pallas_call(
        functools.partial(finish_kernel, domains),
        out_shape=(own_shape, own_shape),
        in_specs=[VM] * 5,
        out_specs=(VM, VM),
        name="finish",
    )(near, key_parts, value_parts, returned, own_terms)
    return attended, grad_query, grad_key, grad_value


def solution(mesh):
    nodes = P(("grp", "dom"), None)
    return jax.shard_map(
        body,
        mesh=mesh,
        in_specs=(
            nodes, nodes, nodes, nodes,
            P(("grp", "dom"), None, None),
            P(("grp", "dom"), None, None, None),
            P(("grp", "dom")),
            nodes,
            P(("grp", "dom"), None, None, None),
        ),
        out_specs=(nodes, nodes, nodes, nodes),
        check_vma=False,
    )
```
